256 devices in a mesh: band: 32 (over y_hi, z, core), fft: 8 (over y_lo, x).
Axes of the slice: x: 4, y: 4 (y_hi: 2, y_lo: 2; y = y_hi * 2 + y_lo), z: 8, core: 2. Of those that a mesh axis runs over, the one named last changes fastest.
Arguments:
- orbitals: float32 [64, 96, 9216], P('band', 'fft'), may hold values from -6 to 6
- owners: int32 [1], replicated, may hold values from 0 to 31
- cutoff_mask: int32 [96, 9216], P(None, 'fft'), may hold values from 0 to 1, as said below
Outputs:
- exchange_local: float32 [64, 96, 9216], P('band', 'fft')
- exchange_block: float32 [2, 96, 9216], P(None, 'fft')
The draws below stay inside these ranges and needn't reach their ends.
Inputs may be any that keep to these rules, and one draw needn't show every extreme that they name: cutoff_mask is 1 exactly at the frequencies whose squared length s(x)^2 + s(y)^2 + s(z)^2 lies between 1 and a cutoff, and 0 elsewhere (0 at frequency (0, 0, 0)); it is unchanged when the sign of any one frequency component is changed.
All inputs are finite; a program needn't handle non-finite values.
Results may differ from the reference program's by a relative error of at most 0.00029.
Values sent between devices are 32-bit elements; how exact they have to be, the bound alone decides.
A program may use at most 128 MiB of HBM per device.

```python
import jax
import jax.numpy as jnp
from jax import lax

NG = 96
NLOC = 2
NBLK = 1
BANDS = 64
BLOCK_BANDS = 2
N_BAND = 32


def draw_cutoff_mask(key, part):
    positions = jnp.arange(NG, dtype=jnp.int32)
    signed = jnp.where(positions <= NG // 2, positions, positions - NG)
    squared = signed[:, None, None] * signed[:, None, None] + signed[None, :, None] * signed[None, :, None] + signed[None, None, :] * signed[None, None, :]
    radius_limit = jax.random.randint(key, (), NG * NG // 90, NG * NG // 6 + 1, dtype=jnp.int32)
    inside = (squared <= radius_limit) & (squared > 0)
    return inside.astype(jnp.int32).reshape(NG, NG * NG)


def level_of(rng, extent, cuts, low, largest):
    def one(position, parts):
        heights = jax.random.uniform(jax.random.fold_in(jax.random.fold_in(rng, 6), position), (parts,), jnp.float32, low / len(cuts), largest / len(cuts))
        return jnp.repeat(jnp.exp(heights), extent[position] // parts).reshape((-1,) + (1,) * (len(extent) - position - 1))

    factor_of = one(*cuts[0])
    for cut in cuts[1:]:
        factor_of = factor_of * one(*cut)
    return factor_of


def noise(stream_key, extent, deviation, reach, split=(), held_as=jnp.bfloat16):
    loudness = level_of(stream_key, extent, split, -0.22, 0.18) if split else 1.0
    result = jax.random.normal(stream_key, extent, jnp.float32) * deviation * loudness
    return jnp.minimum(jnp.maximum(result, -reach), reach).astype(held_as)


def setup_inputs(seed: int = 0) -> dict:
    key_list = jax.random.split(jax.random.key(seed), 4)
    orbitals = noise(key_list[0], (BANDS, NG, NG * NG), 1.0, 6.0, ((0, 32), (1, 8)), jnp.float32)
    owners = jax.random.randint(key_list[1], (NBLK,), 0, N_BAND).astype(jnp.int32)
    cutoff_mask = draw_cutoff_mask(jax.random.fold_in(key_list[3], 71), 0)
    return dict(orbitals=orbitals, owners=owners, cutoff_mask=cutoff_mask)


COULOMB = 400.0
EXCHANGE_MIX = 0.25


def make_kernel(cutoff_mask):
    positions = jnp.arange(NG, dtype=jnp.int32)
    signed = jnp.where(positions <= NG // 2, positions, positions - NG)
    squared = signed[:, None, None] * signed[:, None, None] + signed[None, :, None] * signed[None, :, None] + signed[None, None, :] * signed[None, None, :]
    weights = cutoff_mask.reshape(NG, NG, NG).astype(jnp.float32)
    return COULOMB * weights / jnp.maximum(squared, 1).astype(jnp.float32)


def reference(orbitals, owners, cutoff_mask):
    kernel = make_kernel(cutoff_mask)
    grid = orbitals.reshape(BANDS, NG, NG, NG)
    pieces = []
    for block_index in range(NBLK):
        start = (owners[block_index] * NLOC).astype(jnp.int32)
        pieces.append(lax.dynamic_slice_in_dim(grid, start, NLOC, 0))
    block_orbs = jnp.concatenate(pieces, axis=0)

    def per_band(carry, single):
        density = single[None] * block_orbs
        spectrum = jnp.fft.fftn(density, axes=(1, 2, 3)) * kernel
        potential = jnp.real(jnp.fft.ifftn(spectrum, axes=(1, 2, 3))).astype(jnp.float32)
        local_value = -EXCHANGE_MIX * jnp.sum(block_orbs * potential, axis=0)
        carry = carry - EXCHANGE_MIX * single[None] * potential
        return carry, local_value

    start_total = jnp.zeros((BLOCK_BANDS, NG, NG, NG), jnp.float32)
    block_total, local_values = lax.scan(per_band, start_total, grid)
    return local_values.reshape(BANDS, NG, NG * NG), block_total.reshape(BLOCK_BANDS, NG, NG * NG)
```

```python
import functools
import math

import jax
import jax.numpy as jnp
import numpy as np
from jax import lax
from jax.experimental import pallas as pl
from jax.experimental.pallas import tpu as pltpu
from jax.sharding import PartitionSpec as P

COULOMB = 400.0
EXCHANGE_MIX = 0.25
NG = 96
NL = 2
NX = 12
NF = 8
NZ = 8
ROWS = NL * NX
LANES = NG * NG
CHUNK = NX * NG
QUADS = NG // 4
TILES = 27
PART = 14
MESH = pl.DeviceIdType.MESH
F32 = jnp.float32
BF16 = jnp.bfloat16


def split_const(matrix):
    high = matrix.astype(np.float32).astype(jnp.bfloat16)
    low = (matrix.astype(np.float64) - np.asarray(high, np.float64)).astype(jnp.bfloat16)
    return np.asarray(high), np.asarray(low)


def tables():
    index = np.arange(NG)
    angle = 2.0 * math.pi * (index[:, None] * index[None, :] % NG) / NG
    cas = np.cos(angle) + np.sin(angle)
    pack = np.zeros((4, 128, 4, NG))
    for b in range(4):
        pack[b, :NG, b, :] = cas
    pack = pack.reshape(512, 384)
    pack_h, pack_l = split_const(pack)
    open_h, open_l = split_const(pack.T)
    cas_h, cas_l = split_const(cas)
    zero = np.zeros_like(cas_h)
    left_y = np.concatenate(
        [np.concatenate([cas_h, cas_h], 1), np.concatenate([cas_l, zero], 1)], 0
    )
    both = np.zeros((NL, NG, NF, NL, NX))
    for i in range(NL):
        both[i, :, :, i, :] = cas.reshape(NG, NF, NX)
    both = both.reshape(NL * NG, NF * ROWS)
    fx_h, fx_l = split_const(both)
    bx_h, bx_l = split_const(both.T)
    left_fx = np.concatenate([fx_h, fx_l], 0)
    left_bx = np.concatenate([bx_h, bx_l], 0)
    return [pack_h, pack_l, open_h, open_l, left_y, left_fx, left_bx]


def dot(a, b):
    return lax.dot_general(a, b, (((1,), (0,)), ((), ())), preferred_element_type=F32)


def split(value):
    high = value.astype(BF16)
    low = (value - high.astype(F32)).astype(BF16)
    return high, low


def right_product(value, high, low):
    rows = value.shape[0]
    vh, vl = split(value)
    first = dot(jnp.concatenate([vh, vl], axis=0), high)
    return first[:rows] + first[rows:] + dot(vh, low)


def left_product(left, value):
    rows = left.shape[0] // 2
    vh, vl = split(value)
    first = dot(left, vh)
    return first[:rows] + first[rows:] + dot(left[:rows], vl)


def lane_iota():
    return lax.broadcasted_iota(jnp.int32, (ROWS, 128), 1)


def row_iota():
    return lax.broadcasted_iota(jnp.int32, (ROWS, 128), 0)


def open_quad(c0, c1, c2):
    lane = lane_iota()
    y1 = jnp.where(lane < 32, pltpu.roll(c0, 32, 1), pltpu.roll(c1, 32, 1))
    y2 = jnp.where(lane < 64, pltpu.roll(c1, 64, 1), pltpu.roll(c2, 64, 1))
    return c0, y1, y2, pltpu.roll(c2, 96, 1)


def close_quad(e0, e1, e2, e3):
    lane = lane_iota()
    r1 = pltpu.roll(e1, 96, 1)
    r2 = pltpu.roll(e2, 64, 1)
    r3 = pltpu.roll(e3, 32, 1)
    c0 = jnp.where(lane < 96, e0, r1)
    c1 = jnp.where(lane < 64, r1, r2)
    c2 = jnp.where(lane < 32, r2, r3)
    return c0, c1, c2


def rows_of(ref, lane):
    lane = pl.multiple_of(lane, 128)
    return jnp.concatenate(
        [ref[0, :, pl.ds(lane, 128)], ref[1, :, pl.ds(lane, 128)]], axis=0
    )


def plane_rows(y):
    return pl.ds(pl.multiple_of(y * ROWS, 8), ROWS)


def exchange_kernel(
    orb_ref, blk_ref, coulomb_ref, pack_h, pack_l, open_h, open_l, left_y, left_fx, left_bx,
    local_ref, block_ref,
    orb_u, dup, work, turned, block_u, local_u, send_a, recv_a, send_b, recv_b,
    ssem_a, rsem_a, ssem_b, rsem_b,
):
    me = lax.axis_index("fft")
    barrier = pltpu.get_barrier_semaphore()
    for o in range(1, NF):
        pl.semaphore_signal(
            barrier, inc=1, device_id={"fft": lax.rem(me + o, NF)}, device_id_type=MESH
        )

    def unpack(a, _):
        quad = open_quad(*[rows_of(orb_ref, a * 384 + 128 * k) for k in range(3)])
        for b in range(4):
            orb_u[plane_rows(4 * a + b), :] = quad[b]
        parts = [
            blk_ref[a // 3, pl.ds((a % 3) * 9 + 3 * k, 3)].reshape(ROWS, 128) for k in range(3)
        ]
        quad = open_quad(*parts)
        row = row_iota()
        for b in range(4):
            turn = pltpu.roll(quad[b], NX, 0)
            dup[0, plane_rows(4 * a + b), :] = jnp.where(row < NX, quad[b], turn)
            dup[1, plane_rows(4 * a + b), :] = jnp.where(row < NX, turn, quad[b])
        return 0

    lax.fori_loop(0, QUADS, unpack, 0)
    pl.semaphore_wait(barrier, NF - 1)

    def along_y(source, target):
        def step(k, _):
            pieces = [source[pl.ds(2 * k + s, NG, stride=ROWS), :] for s in range(2)]
            vh, vl = split(jnp.concatenate(pieces, axis=1))
            full = dot(left_y[...], jnp.concatenate([vh, vl], axis=0))
            out = full[:NG] + full[NG:]
            for s in range(2):
                target[pl.ds(2 * k + s, NG, stride=ROWS), :] = out[:, 128 * s : 128 * s + 128]
            return 0

        lax.fori_loop(0, ROWS // 2, step, 0)

    def copy_a(j, peer, slot):
        return pltpu.make_async_remote_copy(
            src_ref=send_a.at[j, peer],
            dst_ref=recv_a.at[j, slot],
            send_sem=ssem_a.at[j, peer],
            recv_sem=rsem_a.at[j, slot],
            device_id={"fft": peer},
            device_id_type=MESH,
        )

    def copy_b(j, peer, slot):
        return pltpu.make_async_remote_copy(
            src_ref=send_b.at[j, peer],
            dst_ref=recv_b.at[j, slot],
            send_sem=ssem_b.at[j, peer],
            recv_sem=rsem_b.at[j, slot],
            device_id={"fft": peer},
            device_id_type=MESH,
        )

    def packed(g):
        pieces = []
        for s in range(3):
            pieces.append(
                jnp.concatenate(
                    [turned[plane_rows(12 * g + 4 * s + b), :] for b in range(4)], axis=1
                )
            )
        return right_product(jnp.concatenate(pieces, axis=0), pack_h[...], pack_l[...])

    def forward(j):
        work[...] = orb_u[...] * dup[j]
        along_y(work, turned)

        def step(o, _):
            peer = lax.rem(me + o, NF)
            out = packed(peer)
            for s in range(3):
                send_a[j, peer, :, 384 * s : 384 * s + 384] = out[ROWS * s : ROWS * s + ROWS]
            copy_a(j, peer, me).start()
            return 0

        lax.fori_loop(1, NF, step, 0)
        out = packed(me)
        for s in range(3):
            recv_a[j, me, :, 384 * s : 384 * s + 384] = out[ROWS * s : ROWS * s + ROWS]

    def middle(j):
        for o in range(1, NF):
            peer = lax.rem(me + o, NF)
            copy_a(j, peer, peer).wait_recv()

        def step(s, _):
            cols = pl.ds(pl.multiple_of(384 * s, 128), 384)
            value = recv_a[j, :, :, cols].reshape(NF * ROWS, 384)
            spectrum = left_product(left_fx[...], value)
            weight = coulomb_ref[:, cols]
            scaled = jnp.concatenate([spectrum[:NG] * weight, spectrum[NG:] * weight], axis=0)
            back = left_product(left_bx[...], scaled)
            send_b[j, :, :, cols] = back.reshape(NF, ROWS, 384)
            return 0

        lax.fori_loop(0, 3, step, 0)
        recv_b[j, me] = send_b[j, me]
        for o in range(1, NF):
            copy_b(j, lax.rem(me + o, NF), me).start()

    def backward(j):
        for o in range(1, NF):
            peer = lax.rem(me + o, NF)
            copy_b(j, peer, peer).wait_recv()

        def step(g, _):
            value = jnp.concatenate(
                [recv_b[j, g, :, 384 * s : 384 * s + 384] for s in range(3)], axis=0
            )
            out = right_product(value, open_h[...], open_l[...])
            for s in range(3):
                for b in range(4):
                    turned[plane_rows(12 * g + 4 * s + b), :] = out[
                        ROWS * s : ROWS * s + ROWS, 128 * b : 128 * b + 128
                    ]
            return 0

        lax.fori_loop(0, NF, step, 0)
        along_y(turned, work)

        def finish(y, _):
            rows = plane_rows(y)
            pot = work[rows, :]
            term = dup[j, rows, :] * pot
            prod = orb_u[rows, :] * pot
            total = prod + pltpu.roll(prod, NX, 0)
            if j == 0:
                local_u[rows, :] = term
                block_u[rows, :] = total
            else:
                local_u[rows, :] = local_u[rows, :] + term
                block_u[rows, :] = jnp.where(row_iota() < NX, block_u[rows, :], total)
            return 0

        lax.fori_loop(0, NG, finish, 0)

    for j in range(NL):
        forward(j)
    for j in range(NL):
        middle(j)
    for j in range(NL):
        backward(j)

    def pack_out(a, _):
        local = close_quad(*[-EXCHANGE_MIX * local_u[plane_rows(4 * a + b), :] for b in range(4)])
        block = close_quad(*[-EXCHANGE_MIX * block_u[plane_rows(4 * a + b), :] for b in range(4)])
        for k in range(3):
            lanes = pl.ds(pl.multiple_of(a * 384 + 128 * k, 128), 128)
            local_ref[0, :, lanes] = local[k][:NX]
            local_ref[1, :, lanes] = local[k][NX:]
            block_ref[a // 3, pl.ds((a % 3) * 9 + 3 * k, 3)] = block[k].reshape(3, 8, 128)
        return 0

    lax.fori_loop(0, QUADS, pack_out, 0)
    for j in range(NL):
        for o in range(1, NF):
            peer = lax.rem(me + o, NF)
            copy_a(j, peer, me).wait_send()
            copy_b(j, peer, me).wait_send()


FAR = (4, 3, 5, 2, 6, 1, 7)


def sum_kernel(
    tiles_in, tiles_out, in_ref, out_ref,
    data, pair, part, gathered, summed, other, total, mate,
    ssem, rsem, zs_sem, zr_sem, gs_sem, gr_sem, ms_sem, mr_sem,
):
    band = lax.axis_index("band")
    core = lax.rem(band, 2)
    z = lax.rem(band // 2, NZ)
    yh = band // (2 * NZ)
    mate_core = 1 - core
    mate_band = band + 1 - 2 * core
    y_band = lax.rem(band + 2 * NZ, 4 * NZ)

    def z_band(other_z):
        return (yh * NZ + other_z) * 2 + core

    barrier = pltpu.get_barrier_semaphore()
    peers = [mate_band, y_band] + [z_band(lax.rem(z + o, NZ)) for o in range(1, NZ)]
    for peer in peers:
        pl.semaphore_signal(barrier, inc=1, device_id={"band": peer}, device_id_type=MESH)

    if tiles_in:
        source = in_ref
    else:
        source = data

        def load(c, _):
            value = rows_of(in_ref, c * 128)
            data[c // 9, pl.ds((c % 9) * 3, 3)] = value.reshape(3, 8, 128)
            return 0

        lax.fori_loop(0, 72, load, 0)
    pl.semaphore_wait(barrier, len(peers))

    def remote(src, dst, send, recv, peer):
        return pltpu.make_async_remote_copy(
            src_ref=src, dst_ref=dst, send_sem=send, recv_sem=recv,
            device_id={"band": peer}, device_id_type=MESH,
        )

    first = remote(
        source.at[:, pl.ds(13 * mate_core, PART)], pair, ssem.at[0], rsem.at[0], mate_band
    )
    first.start()
    first.wait_recv()

    def add_pair(k, _):
        part[k] = source[k, pl.ds(13 * core, PART)] + pair[k]
        return 0

    lax.fori_loop(0, NZ, add_pair, 0)

    def scatter(peer, slot):
        return remote(part.at[peer], gathered.at[slot], zs_sem.at[peer], zr_sem.at[slot], z_band(peer))

    for o in FAR:
        scatter(lax.rem(z + o, NZ), z).start()
    gathered[z] = part[z]
    for o in FAR:
        peer = lax.rem(z + o, NZ)
        scatter(peer, peer).wait_recv()
    value = gathered[0]
    for k in range(1, NZ):
        value = value + gathered[k]
    summed[...] = value
    second = remote(summed, other, ssem.at[1], rsem.at[1], y_band)
    second.start()
    second.wait_recv()
    total[z] = summed[...] + other[...]

    def spread(peer, slot):
        return remote(total.at[slot], total.at[slot], gs_sem.at[peer], gr_sem.at[slot], z_band(peer))

    def to_mate(slot):
        return remote(total.at[slot], mate.at[slot], ms_sem.at[slot], mr_sem.at[slot], mate_band)

    for o in FAR:
        spread(lax.rem(z + o, NZ), z).start()
    to_mate(z).start()
    for o in (1, 7, 2, 6, 3, 5, 4):
        peer = lax.rem(z + o, NZ)
        spread(peer, peer).wait_recv()
        to_mate(peer).start()
    for o in (0, 1, 7, 2, 6, 3, 5, 4):
        to_mate(lax.rem(z + o, NZ)).wait_recv()

    target = out_ref if tiles_out else data

    def merge(k, _):
        target[k, pl.ds(13 * core, PART)] = total[k]
        target[k, pl.ds(13 * mate_core, PART)] = mate[k]
        return 0

    first.wait_send()
    lax.fori_loop(0, NZ, merge, 0)
    if not tiles_out:

        def store(c, _):
            value = data[c // 9, pl.ds((c % 9) * 3, 3)].reshape(ROWS, 128)
            lanes = pl.ds(pl.multiple_of(c * 128, 128), 128)
            out_ref[0, :, lanes] = value[:NX]
            out_ref[1, :, lanes] = value[NX:]
            return 0

        lax.fori_loop(0, 72, store, 0)
    second.wait_send()
    for o in FAR:
        peer = lax.rem(z + o, NZ)
        scatter(peer, z).wait_send()
        spread(peer, z).wait_send()
    for o in range(NZ):
        to_mate(lax.rem(z + o, NZ)).wait_send()


TILE_SHAPE = (NZ, TILES, 8, 128)
FLAT_SHAPE = (NL, NX, LANES)


def all_sum(value, tiles_in, tiles_out, collective_id):
    vmem = pl.BlockSpec(memory_space=pltpu.VMEM)
    shape = TILE_SHAPE if tiles_out else FLAT_SHAPE
    piece = pltpu.VMEM((NZ, PART, 8, 128), F32)
    single = pltpu.VMEM((PART, 8, 128), F32)
    dma = pltpu.SemaphoreType.DMA
    return pl.pallas_call(
        functools.partial(sum_kernel, tiles_in, tiles_out),
        out_shape=jax.ShapeDtypeStruct(shape, F32),
        in_specs=[vmem],
        out_specs=vmem,
        scratch_shapes=[
            pltpu.VMEM(TILE_SHAPE, F32), piece, piece, piece, single, single, piece, piece,
            dma((2,)), dma((2,)), dma((NZ,)), dma((NZ,)), dma((NZ,)), dma((NZ,)),
            dma((NZ,)), dma((NZ,)),
        ],
        compiler_params=pltpu.CompilerParams(
            collective_id=collective_id, has_side_effects=True, vmem_limit_bytes=48 << 20
        ),
    )(value)


def exchange(orbitals, block, coulomb):
    vmem = pl.BlockSpec(memory_space=pltpu.VMEM)
    constants = [jnp.asarray(t) for t in tables()]
    plane = pltpu.VMEM((NG * ROWS, 128), F32)
    buffer = pltpu.VMEM((NL, NF, ROWS, CHUNK), F32)
    dma = pltpu.SemaphoreType.DMA
    return pl.pallas_call(
        exchange_kernel,
        out_shape=(
            jax.ShapeDtypeStruct(FLAT_SHAPE, F32),
            jax.ShapeDtypeStruct(TILE_SHAPE, F32),
        ),
        in_specs=[vmem] * 10,
        out_specs=(vmem, vmem),
        scratch_shapes=[
            plane, pltpu.VMEM((NL, NG * ROWS, 128), F32), plane, plane, plane, plane,
            buffer, buffer, buffer, buffer,
            dma((NL, NF)), dma((NL, NF)), dma((NL, NF)), dma((NL, NF)),
        ],
        compiler_params=pltpu.CompilerParams(
            collective_id=1, has_side_effects=True, vmem_limit_bytes=60 << 20
        ),
    )(orbitals, block, coulomb, *constants)


def coulomb_table(cutoff_mask):
    positions = jnp.arange(NG, dtype=jnp.int32)
    signed = jnp.where(positions <= NG // 2, positions, positions - NG)
    signed_y = lax.dynamic_slice_in_dim(signed, lax.axis_index("fft") * NX, NX)
    flat = jnp.repeat(signed_y * signed_y, NG) + jnp.tile(signed * signed, NX)
    squared = signed[:, None] * signed[:, None] + flat[None, :]
    weights = cutoff_mask.astype(F32)
    return COULOMB * weights / jnp.maximum(squared, 1).astype(F32) / float(NG**3)


def per_device(orbitals, owners, cutoff_mask):
    mine = lax.axis_index("band") == owners[0]
    kept = jnp.where(mine, orbitals, 0.0)
    block = all_sum(kept, False, True, 0)
    local, terms = exchange(orbitals, block, coulomb_table(cutoff_mask))
    return local, all_sum(terms, True, False, 2)


def solution(mesh):
    in_specs = (P("band", "fft", None), P(), P(None, "fft"))
    out_specs = (P("band", "fft", None), P(None, "fft", None))
    return jax.shard_map(
        per_device, mesh=mesh, in_specs=in_specs, out_specs=out_specs, check_vma=False
    )
```

```python
import math

import jax
import jax.numpy as jnp
import numpy as np
from jax import lax
from jax.experimental import pallas as pl
from jax.experimental.pallas import tpu as pltpu
from jax.sharding import PartitionSpec as P

COULOMB = 400.0
EXCHANGE_MIX = 0.25
NG = 96
NL = 2
NX = 12
NF = 8
NZ = 8
NT = 3
LANES = NG * NG
CHUNK = NX * NG
QUADS = NG // 4
PLANES = NG * 8
PART = 5
MESH = pl.DeviceIdType.MESH
F32 = jnp.float32
BF16 = jnp.bfloat16
FAR = (4, 3, 5, 2, 6, 1, 7)
NEAR = (1, 7, 2, 6, 3, 5, 4)


def split_const(matrix):
    high = matrix.astype(np.float32).astype(jnp.bfloat16)
    low = (matrix.astype(np.float64) - np.asarray(high, np.float64)).astype(jnp.bfloat16)
    return np.asarray(high), np.asarray(low)


def tables():
    index = np.arange(NG)
    angle = 2.0 * math.pi * (index[:, None] * index[None, :] % NG) / NG
    cas = np.cos(angle) + np.sin(angle)
    cas_h, cas_l = split_const(cas)
    zero = np.zeros_like(cas_h)
    left_y = np.concatenate(
        [np.concatenate([cas_h, cas_h], 1), np.concatenate([cas_l, zero], 1)], 0
    )
    right_z = np.zeros((256, 256), cas_h.dtype)
    right_z[:NG, :NG] = cas_h
    right_z[128 : 128 + NG, :NG] = cas_h
    right_z[:NG, 128 : 128 + NG] = cas_l
    both = np.zeros((NL, NG, NT, NF, NL, 4))
    for i in range(NL):
        both[i, :, :, :, i, :] = cas.reshape(NG, NF, NT, 4).transpose(0, 2, 1, 3)
    both = both.reshape(NL * NG, NL * NG)
    left_fx = np.concatenate(split_const(both), 0)
    left_bx = np.concatenate(split_const(both.T), 0)
    signed = np.where(index <= NG // 2, index, index - NG)
    lane_y = np.tile(np.repeat(np.arange(NX), NG)[None], (8, 1)).astype(np.int32)
    lane_z = np.tile(np.tile(signed * signed, NX)[None], (8, 1)).astype(np.int32)
    row_x = np.tile((signed * signed)[:, None], (1, 128)).astype(np.int32)
    return [left_y, right_z, left_fx, left_bx, lane_y, lane_z, row_x]


def dot(a, b):
    return lax.dot_general(a, b, (((1,), (0,)), ((), ())), preferred_element_type=F32)


def split(value):
    high = value.astype(BF16)
    low = (value - high.astype(F32)).astype(BF16)
    return high, low


def left_product(left, value):
    rows = left.shape[0] // 2
    vh, vl = split(value)
    first = dot(left, vh)
    return first[:rows] + first[rows:] + dot(left[:rows], vl)


def open_quad(c0, c1, c2):
    lane = lax.broadcasted_iota(jnp.int32, (8, 128), 1)
    y1 = jnp.where(lane < 32, pltpu.roll(c0, 32, 1), pltpu.roll(c1, 32, 1))
    y2 = jnp.where(lane < 64, pltpu.roll(c1, 64, 1), pltpu.roll(c2, 64, 1))
    return c0, y1, y2, pltpu.roll(c2, 96, 1)


def close_quad(e0, e1, e2, e3):
    lane = lax.broadcasted_iota(jnp.int32, (8, 128), 1)
    r1 = pltpu.roll(e1, 96, 1)
    r2 = pltpu.roll(e2, 64, 1)
    r3 = pltpu.roll(e3, 32, 1)
    c0 = jnp.where(lane < 96, e0, r1)
    c1 = jnp.where(lane < 64, r1, r2)
    c2 = jnp.where(lane < 32, r2, r3)
    return c0, c1, c2


def plane(y):
    return pl.ds(pl.multiple_of(y * 8, 8), 8)


def across(row):
    return pl.ds(row, NG, stride=8)


def kernel(
    orb_ref, keep_ref, mask_ref, left_y, right_z, left_fx, left_bx, lane_y, lane_z, row_x,
    local_ref, block_ref,
    coulomb, orb_t, source, full, orb_u, blk_u, turned, local_u, block_u,
    send_a, recv_a, send_b, recv_b, pair, part, gathered, summed, other, total, mate,
    sa_sem, ra_sem, sb_sem, rb_sem, ps_sem, pr_sem, ys_sem, yr_sem,
    zs_sem, zr_sem, gs_sem, gr_sem, ms_sem, mr_sem,
):
    me = lax.axis_index("fft")
    band = lax.axis_index("band")
    core = lax.rem(band, 2)
    z = lax.rem(band // 2, NZ)
    yh = band // (2 * NZ)
    mate_band = band + 1 - 2 * core
    y_band = lax.rem(band + 2 * NZ, 4 * NZ)

    def z_band(other_z):
        return (yh * NZ + other_z) * 2 + core

    def turn(o):
        return lax.rem(me + o, NF)

    def turn_z(o):
        return lax.rem(z + o, NZ)

    barrier = pltpu.get_barrier_semaphore()
    devices = [{"fft": turn(o)} for o in range(1, NF)]
    devices += [{"band": mate_band}, {"band": y_band}]
    devices += [{"band": z_band(turn_z(o))} for o in range(1, NZ)]
    for device in devices:
        pl.semaphore_signal(barrier, inc=1, device_id=device, device_id_type=MESH)

    def remote(src, dst, send, recv, device):
        return pltpu.make_async_remote_copy(
            src_ref=src, dst_ref=dst, send_sem=send, recv_sem=recv,
            device_id=device, device_id_type=MESH,
        )

    def copy_a(j, t, peer, slot):
        return remote(
            send_a.at[j, t, peer], recv_a.at[j, t, slot],
            sa_sem.at[j, t, peer], ra_sem.at[j, t, slot], {"fft": peer},
        )

    def copy_b(j, t, peer, slot):
        return remote(
            send_b.at[j, t, peer], recv_b.at[j, t, slot],
            sb_sem.at[j, t, peer], rb_sem.at[j, t, slot], {"fft": peer},
        )

    def to_pair(q, t):
        return remote(
            source.at[q, t, :, pl.ds(4 * (1 - core), PART)], pair.at[q, t],
            ps_sem.at[q, t], pr_sem.at[q, t], {"band": mate_band},
        )

    def scatter(q, t, peer, slot):
        return remote(
            part.at[q, t, peer], gathered.at[q, t, slot],
            zs_sem.at[q, t, peer], zr_sem.at[q, t, slot], {"band": z_band(peer)},
        )

    def to_y(q, t):
        return remote(
            summed.at[q, t], other.at[q, t], ys_sem.at[q, t], yr_sem.at[q, t], {"band": y_band}
        )

    def spread(q, t, peer, slot):
        return remote(
            total.at[q, t, slot], total.at[q, t, slot],
            gs_sem.at[q, t, peer], gr_sem.at[q, t, slot], {"band": z_band(peer)},
        )

    def to_mate(q, t, slot):
        return remote(
            total.at[q, t, slot], mate.at[q, t, slot],
            ms_sem.at[q, t, slot], mr_sem.at[q, t, slot], {"band": mate_band},
        )

    def sum_a(q, t):
        to_pair(q, t).start()

    def sum_b(q, t):
        to_pair(q, t).wait_recv()

        def step(k, _):
            part[q, t, k] = source[q, t, k, pl.ds(4 * core, PART)] + pair[q, t, k]
            return 0

        lax.fori_loop(0, NZ, step, 0, unroll=2)
        for o in FAR:
            scatter(q, t, turn_z(o), z).start()
        gathered[q, t, z] = part[q, t, z]

    def sum_c(q, t):
        for o in FAR:
            scatter(q, t, turn_z(o), turn_z(o)).wait_recv()
        value = gathered[q, t, 0]
        for k in range(1, NZ):
            value = value + gathered[q, t, k]
        summed[q, t] = value
        to_y(q, t).start()

    def sum_d(q, t):
        to_y(q, t).wait_recv()
        total[q, t, z] = summed[q, t] + other[q, t]
        for o in FAR:
            spread(q, t, turn_z(o), z).start()
        to_mate(q, t, z).start()

    def sum_e(q, t):
        for o in NEAR:
            spread(q, t, turn_z(o), turn_z(o)).wait_recv()
            to_mate(q, t, turn_z(o)).start()

    def sum_f(q, t):
        for o in (0,) + NEAR:
            to_mate(q, t, turn_z(o)).wait_recv()

        def step(k, _):
            full[q, t, k, pl.ds(4 * core, PART)] = total[q, t, k]
            full[q, t, k, pl.ds(4 * (1 - core), PART)] = mate[q, t, k]
            return 0

        lax.fori_loop(0, NZ, step, 0, unroll=2)

    def load_tiles(c, _):
        lanes = pl.ds(pl.multiple_of(c * 128, 128), 128)
        rows0, rows1 = orb_ref[0, :, lanes], orb_ref[1, :, lanes]
        keep = keep_ref[...]
        for t in range(NT):
            tile = jnp.concatenate([rows0[4 * t : 4 * t + 4], rows1[4 * t : 4 * t + 4]], axis=0)
            orb_t[t, c // 9, c % 9] = tile
            source[0, t, c // 9, c % 9] = tile * keep
        return 0

    lax.fori_loop(0, LANES // 128, load_tiles, 0, unroll=4)
    pl.semaphore_wait(barrier, len(devices))
    for t in range(NT):
        sum_a(0, t)

    low = lax.rem(me, NF) * NX + lane_y[...]
    low = jnp.where(low <= NG // 2, low, low - NG)
    flat = low * low + lane_z[...]

    def coulomb_rows(k, _):
        rows = pl.ds(pl.multiple_of(8 * k, 8), 8)
        squared = jnp.concatenate([row_x[rows, :]] * 9, axis=1) + flat
        weight = mask_ref[rows, :].astype(F32)
        scale = -EXCHANGE_MIX * COULOMB / float(NG**3)
        coulomb[rows, :] = scale * weight / jnp.maximum(squared, 1).astype(F32)
        return 0

    lax.fori_loop(0, NG // 8, coulomb_rows, 0)
    for t in range(NT):
        sum_b(0, t)

    def open_orb(a, _):
        for t in range(NT):
            quad = open_quad(*[orb_t[t, a // 3, (a % 3) * 3 + k] for k in range(3)])
            for b in range(4):
                orb_u[t, plane(4 * a + b), :] = quad[b]
        return 0

    lax.fori_loop(0, QUADS, open_orb, 0, unroll=2)
    for t in range(NT):
        sum_c(0, t)
    for t in range(NT):
        sum_d(0, t)

    def open_blk(t):
        def step(a, _):
            quad = open_quad(*[full[0, t, a // 3, (a % 3) * 3 + k] for k in range(3)])
            for b in range(4):
                blk_u[t, plane(4 * a + b), :] = quad[b]
            return 0

        lax.fori_loop(0, QUADS, step, 0, unroll=4)

    def transform_y(p0, p1):
        vh, vl = split(jnp.concatenate([p0, p1], axis=1))
        out = dot(left_y[...], jnp.concatenate([vh, vl], axis=0))
        out = out[:NG] + out[NG:]
        return out[:, :128], out[:, 128:]

    def transform_z(value):
        vh, vl = split(value)
        out = dot(jnp.concatenate([vh, vl], axis=1), right_z[...])
        return out[:, :128] + out[:, 128:]

    def forward(j, t):
        def rows(s, _):
            blk = blk_u[t, across(4 * j + s), :]
            out0, out1 = transform_y(
                orb_u[t, across(s), :] * blk, orb_u[t, across(4 + s), :] * blk
            )
            turned[across(s), :] = out0
            turned[across(4 + s), :] = out1
            return 0

        lax.fori_loop(0, 4, rows, 0, unroll=2)

        def half(h, _):
            out = transform_z(turned[pl.ds(pl.multiple_of(384 * h, 8), 384), :])
            for g in range(4):
                for s in range(3):
                    base = 96 * g + 32 * s
                    tiles = close_quad(*[out[base + 8 * b : base + 8 * b + 8] for b in range(4)])
                    for k in range(3):
                        lane = 384 * s + 128 * k
                        send_a[j, t, 4 * h + g, :, lane : lane + 128] = tiles[k]
            return 0

        lax.fori_loop(0, 2, half, 0)
        for o in range(1, NF):
            copy_a(j, t, turn(o), me).start()
        recv_a[j, t, me] = send_a[j, t, me]

    def middle(j):
        for t in range(NT):
            for o in range(1, NF):
                copy_a(j, t, turn(o), turn(o)).wait_recv()

        def step(s, _):
            cols = pl.ds(pl.multiple_of(384 * s, 128), 384)
            value = recv_a[j, :, :, :, cols].reshape(NL * NG, 384)
            spectrum = left_product(left_fx[...], value)
            weight = coulomb[:, cols]
            scaled = jnp.concatenate([spectrum[:NG] * weight, spectrum[NG:] * weight], axis=0)
            back = left_product(left_bx[...], scaled)
            send_b[j, :, :, :, cols] = back.reshape(NT, NF, 8, 384)
            return 0

        lax.fori_loop(0, 3, step, 0)
        for t in range(NT):
            for o in range(1, NF):
                copy_b(j, t, turn(o), me).start()
            recv_b[j, t, me] = send_b[j, t, me]

    def backward(j, t):
        for o in range(1, NF):
            copy_b(j, t, turn(o), turn(o)).wait_recv()

        def half(h, _):
            planes = []
            for g in range(4):
                for s in range(3):
                    planes += open_quad(
                        *[
                            recv_b[j, t, 4 * h + g, :, 384 * s + 128 * k : 384 * s + 128 * k + 128]
                            for k in range(3)
                        ]
                    )
            out = transform_z(jnp.concatenate(planes, axis=0))
            turned[pl.ds(pl.multiple_of(384 * h, 8), 384), :] = out
            return 0

        lax.fori_loop(0, 2, half, 0)

        def rows(s, _):
            pot0, pot1 = transform_y(turned[across(s), :], turned[across(4 + s), :])
            blk = blk_u[t, across(4 * j + s), :]
            term0, term1 = blk * pot0, blk * pot1
            if j > 0:
                term0 = local_u[t, across(s), :] + term0
                term1 = local_u[t, across(4 + s), :] + term1
            local_u[t, across(s), :] = term0
            local_u[t, across(4 + s), :] = term1
            block_u[t, across(4 * j + s), :] = (
                orb_u[t, across(s), :] * pot0 + orb_u[t, across(4 + s), :] * pot1
            )
            return 0

        lax.fori_loop(0, 4, rows, 0, unroll=2)

    def close_block(t):
        def step(a, _):
            tiles = close_quad(*[block_u[t, plane(4 * a + b), :] for b in range(4)])
            for k in range(3):
                source[1, t, a // 3, (a % 3) * 3 + k] = tiles[k]
            return 0

        lax.fori_loop(0, QUADS, step, 0, unroll=4)

    def write(ref, t, column, tile):
        lanes = pl.ds(pl.multiple_of(column * 128, 128), 128)
        ref[0, 4 * t : 4 * t + 4, lanes] = tile[:4]
        ref[1, 4 * t : 4 * t + 4, lanes] = tile[4:]

    def write_local(a, _):
        for t in range(NT):
            tiles = close_quad(*[local_u[t, plane(4 * a + b), :] for b in range(4)])
            for k in range(3):
                write(local_ref, t, 3 * a + k, tiles[k])
        return 0

    def write_block(t):
        def step(c, _):
            write(block_ref, t, c, full[1, t, c // 9, c % 9])
            return 0

        lax.fori_loop(0, LANES // 128, step, 0, unroll=4)

    for t in range(NT):
        sum_e(0, t)
        sum_f(0, t)
        open_blk(t)
        forward(0, t)
    for t in range(NT):
        forward(1, t)
    middle(0)
    middle(1)
    for t in range(NT):
        backward(0, t)
    backward(1, 0)
    close_block(0)
    sum_a(1, 0)
    backward(1, 1)
    close_block(1)
    sum_a(1, 1)
    sum_b(1, 0)
    backward(1, 2)
    close_block(2)
    sum_a(1, 2)
    sum_b(1, 1)
    sum_c(1, 0)
    sum_b(1, 2)
    lax.fori_loop(0, QUADS, write_local, 0, unroll=2)
    sum_d(1, 0)
    sum_c(1, 1)
    sum_d(1, 1)
    sum_c(1, 2)
    sum_d(1, 2)
    for t in range(NT):
        sum_e(1, t)
    for t in range(NT):
        sum_f(1, t)
        write_block(t)
    for t in range(NT):
        for j in range(NL):
            for o in range(1, NF):
                copy_a(j, t, turn(o), me).wait_send()
                copy_b(j, t, turn(o), me).wait_send()
            to_pair(j, t).wait_send()
            to_y(j, t).wait_send()
            to_mate(j, t, z).wait_send()
            for o in range(1, NZ):
                scatter(j, t, turn_z(o), z).wait_send()
                spread(j, t, turn_z(o), z).wait_send()
                to_mate(j, t, turn_z(o)).wait_send()


def per_device(orbitals, owners, cutoff_mask):
    mine = lax.axis_index("band") == owners[0]
    keep = jnp.broadcast_to(mine.astype(F32), (8, 128))
    vmem = pl.BlockSpec(memory_space=pltpu.VMEM)
    dma = pltpu.SemaphoreType.DMA

    def buffer(*shape):
        return pltpu.VMEM(shape, F32)

    planes = buffer(NT, PLANES, 128)
    tiles = buffer(2, NT, NZ, 9, 8, 128)
    pieces = buffer(2, NT, NZ, PART, 8, 128)
    single = buffer(2, NT, PART, 8, 128)
    grid = buffer(NL, NT, NF, 8, CHUNK)
    constants = [jnp.asarray(t) for t in tables()]
    flat = jax.ShapeDtypeStruct((NL, NX, LANES), F32)
    many = dma((2, NT, NF))
    few = dma((2, NT))
    return pl.pallas_call(
        kernel,
        out_shape=(flat, flat),
        in_specs=[vmem] * (3 + len(constants)),
        out_specs=(vmem, vmem),
        scratch_shapes=[
            buffer(NG, CHUNK), buffer(NT, NZ, 9, 8, 128), tiles, tiles, planes, planes,
            buffer(PLANES, 128), planes, planes, grid, grid, grid, grid,
            pieces, pieces, pieces, single, single, pieces, pieces,
            many, many, many, many, few, few, few, few, many, many, many, many, many, many,
        ],
        compiler_params=pltpu.CompilerParams(
            collective_id=0, has_side_effects=True, vmem_limit_bytes=60 << 20
        ),
    )(orbitals, keep, cutoff_mask, *constants)


def solution(mesh):
    in_specs = (P("band", "fft", None), P(), P(None, "fft"))
    out_specs = (P("band", "fft", None), P(None, "fft", None))
    return jax.shard_map(
        per_device, mesh=mesh, in_specs=in_specs, out_specs=out_specs, check_vma=False
    )
```

```python
import math

import jax
import jax.numpy as jnp
import numpy as np
from jax import lax
from jax.experimental import pallas as pl
from jax.experimental.pallas import tpu as pltpu
from jax.sharding import PartitionSpec as P

COULOMB = 400.0
EXCHANGE_MIX = 0.25
NG = 96
NL = 2
NX = 12
NF = 8
NZ = 8
NT = 3
LANES = NG * NG
CHUNK = NX * NG
QUADS = NG // 4
PLANES = NG * 8
PART = 5
MESH = pl.DeviceIdType.MESH
F32 = jnp.float32
BF16 = jnp.bfloat16
FAR = (4, 3, 5, 2, 6, 1, 7)
NEAR = (1, 7, 2, 6, 3, 5, 4)


def split_const(matrix):
    high = matrix.astype(np.float32).astype(jnp.bfloat16)
    low = (matrix.astype(np.float64) - np.asarray(high, np.float64)).astype(jnp.bfloat16)
    return np.asarray(high), np.asarray(low)


def tables():
    index = np.arange(NG)
    angle = 2.0 * math.pi * (index[:, None] * index[None, :] % NG) / NG
    cas = np.cos(angle) + np.sin(angle)
    cas_h, cas_l = split_const(cas)
    zero = np.zeros_like(cas_h)
    left_y = np.concatenate(
        [np.concatenate([cas_h, cas_h], 1), np.concatenate([cas_l, zero], 1)], 0
    )
    right_z = np.zeros((256, 256), cas_h.dtype)
    right_z[:NG, :NG] = cas_h
    right_z[128 : 128 + NG, :NG] = cas_h
    right_z[:NG, 128 : 128 + NG] = cas_l
    both = np.zeros((NL, NG, NT, NF, 4, NL))
    for i in range(NL):
        both[i, :, :, :, :, i] = cas.reshape(NG, NF, NT, 4).transpose(0, 2, 1, 3)
    both = both.reshape(NL * NG, NL * NG)
    left_fx = np.concatenate(split_const(both), 0)
    left_bx = np.concatenate(split_const(both.T), 0)
    signed = np.where(index <= NG // 2, index, index - NG)
    lane_y = np.tile(np.repeat(np.arange(NX), NG)[None], (8, 1)).astype(np.int32)
    lane_z = np.tile(np.tile(signed * signed, NX)[None], (8, 1)).astype(np.int32)
    row_x = np.tile((signed * signed)[:, None], (1, 128)).astype(np.int32)
    return [left_y, right_z, left_fx, left_bx, lane_y, lane_z, row_x]


def dot(a, b):
    return lax.dot_general(a, b, (((1,), (0,)), ((), ())), preferred_element_type=F32)


def split(value):
    high = value.astype(BF16)
    low = (value - high.astype(F32)).astype(BF16)
    return high, low


def left_product(left, value):
    rows = left.shape[0] // 2
    vh, vl = split(value)
    first = dot(left, vh)
    return first[:rows] + first[rows:] + dot(left[:rows], vl)


def open_quad(c0, c1, c2):
    lane = lax.broadcasted_iota(jnp.int32, (8, 128), 1)
    y1 = jnp.where(lane < 32, pltpu.roll(c0, 32, 1), pltpu.roll(c1, 32, 1))
    y2 = jnp.where(lane < 64, pltpu.roll(c1, 64, 1), pltpu.roll(c2, 64, 1))
    return c0, y1, y2, pltpu.roll(c2, 96, 1)


def close_quad(e0, e1, e2, e3):
    lane = lax.broadcasted_iota(jnp.int32, (8, 128), 1)
    r1 = pltpu.roll(e1, 96, 1)
    r2 = pltpu.roll(e2, 64, 1)
    r3 = pltpu.roll(e3, 32, 1)
    c0 = jnp.where(lane < 96, e0, r1)
    c1 = jnp.where(lane < 64, r1, r2)
    c2 = jnp.where(lane < 32, r2, r3)
    return c0, c1, c2


def plane(y):
    return pl.ds(pl.multiple_of(y * 8, 8), 8)


def across(row):
    return pl.ds(row, NG, stride=8)


def kernel(
    orb_ref, owner_ref, mask_ref, left_y, right_z, left_fx, left_bx, lane_y, lane_z, row_x,
    local_ref, block_ref,
    coulomb, orb_t, source, full, orb_u, blk_u, turned, local_u, block_u,
    send_a, recv_a, send_b, recv_b, pair, part, gathered, summed, other, total, mate,
    sa_sem, ra_sem, sb_sem, rb_sem, ps_sem, pr_sem, ys_sem, yr_sem,
    zs_sem, zr_sem, gs_sem, gr_sem, ms_sem, mr_sem,
):
    me = lax.axis_index("fft")
    band = lax.axis_index("band")
    core = lax.rem(band, 2)
    z = lax.rem(band // 2, NZ)
    yh = band // (2 * NZ)
    mate_band = band + 1 - 2 * core
    y_band = lax.rem(band + 2 * NZ, 4 * NZ)

    def z_band(other_z):
        return (yh * NZ + other_z) * 2 + core

    def turn(o):
        return lax.rem(me + o, NF)

    def turn_z(o):
        return lax.rem(z + o, NZ)

    barrier = pltpu.get_barrier_semaphore()
    devices = [{"fft": turn(o)} for o in range(1, NF)]
    devices += [{"band": mate_band}, {"band": y_band}]
    devices += [{"band": z_band(turn_z(o))} for o in range(1, NZ)]
    for device in devices:
        pl.semaphore_signal(barrier, inc=1, device_id=device, device_id_type=MESH)

    def remote(src, dst, send, recv, device):
        return pltpu.make_async_remote_copy(
            src_ref=src, dst_ref=dst, send_sem=send, recv_sem=recv,
            device_id=device, device_id_type=MESH,
        )

    def copy_a(j, t, peer, slot):
        return remote(
            send_a.at[j, t, peer], recv_a.at[j, t, slot],
            sa_sem.at[j, t, peer], ra_sem.at[j, t, slot], {"fft": peer},
        )

    def copy_b(j, t, peer, slot):
        return remote(
            send_b.at[j, t, peer], recv_b.at[j, t, slot],
            sb_sem.at[j, t, peer], rb_sem.at[j, t, slot], {"fft": peer},
        )

    def to_pair(q, t):
        return remote(
            source.at[q, t, :, pl.ds(4 * (1 - core), PART)], pair.at[q, t],
            ps_sem.at[q, t], pr_sem.at[q, t], {"band": mate_band},
        )

    def scatter(q, t, peer, slot):
        return remote(
            part.at[q, t, peer], gathered.at[q, t, slot],
            zs_sem.at[q, t, peer], zr_sem.at[q, t, slot], {"band": z_band(peer)},
        )

    def to_y(q, t):
        return remote(
            summed.at[q, t], other.at[q, t], ys_sem.at[q, t], yr_sem.at[q, t], {"band": y_band}
        )

    def spread(q, t, peer, slot):
        return remote(
            total.at[q, t, slot], total.at[q, t, slot],
            gs_sem.at[q, t, peer], gr_sem.at[q, t, slot], {"band": z_band(peer)},
        )

    def to_mate(q, t, slot):
        return remote(
            total.at[q, t, slot], mate.at[q, t, slot],
            ms_sem.at[q, t, slot], mr_sem.at[q, t, slot], {"band": mate_band},
        )

    def sum_a(q, t):
        to_pair(q, t).start()

    def sum_b(q, t):
        to_pair(q, t).wait_recv()

        def step(k, _):
            part[q, t, k] = source[q, t, k, pl.ds(4 * core, PART)] + pair[q, t, k]
            return 0

        lax.fori_loop(0, NZ, step, 0, unroll=2)
        for o in FAR:
            scatter(q, t, turn_z(o), z).start()
        gathered[q, t, z] = part[q, t, z]

    def sum_c(q, t):
        for o in FAR:
            scatter(q, t, turn_z(o), turn_z(o)).wait_recv()
        value = gathered[q, t, 0]
        for k in range(1, NZ):
            value = value + gathered[q, t, k]
        summed[q, t] = value
        to_y(q, t).start()

    def sum_d(q, t):
        to_y(q, t).wait_recv()
        total[q, t, z] = summed[q, t] + other[q, t]
        for o in FAR:
            spread(q, t, turn_z(o), z).start()
        to_mate(q, t, z).start()

    def sum_e(q, t):
        for o in NEAR:
            spread(q, t, turn_z(o), turn_z(o)).wait_recv()
            to_mate(q, t, turn_z(o)).start()

    def sum_f(q, t):
        for o in (0,) + NEAR:
            to_mate(q, t, turn_z(o)).wait_recv()

        def step(k, _):
            full[q, t, k, pl.ds(4 * core, PART)] = total[q, t, k]
            full[q, t, k, pl.ds(4 * (1 - core), PART)] = mate[q, t, k]
            return 0

        lax.fori_loop(0, NZ, step, 0, unroll=2)

    mine = jnp.broadcast_to(owner_ref[0], (8, 128)) == band

    def load_tiles(c, _):
        lanes = pl.ds(pl.multiple_of(c * 128, 128), 128)
        for t in range(NT):
            tile = orb_ref[4 * t : 4 * t + 4, :, lanes].reshape(8, 128)
            orb_t[t, c // 9, c % 9] = tile
            source[0, t, c // 9, c % 9] = jnp.where(mine, tile, 0.0)
        return 0

    lax.fori_loop(0, LANES // 128, load_tiles, 0, unroll=4)
    pl.semaphore_wait(barrier, len(devices))
    for t in range(NT):
        sum_a(0, t)

    low = lax.rem(me, NF) * NX + lane_y[...]
    low = jnp.where(low <= NG // 2, low, low - NG)
    flat = low * low + lane_z[...]

    def coulomb_rows(k, _):
        rows = pl.ds(pl.multiple_of(8 * k, 8), 8)
        squared = jnp.concatenate([row_x[rows, :]] * 9, axis=1) + flat
        weight = mask_ref[rows, :].astype(F32)
        scale = -EXCHANGE_MIX * COULOMB / float(NG**3)
        coulomb[rows, :] = scale * weight / jnp.maximum(squared, 1).astype(F32)
        return 0

    lax.fori_loop(0, NG // 8, coulomb_rows, 0)
    for t in range(NT):
        sum_b(0, t)

    def open_orb(a, _):
        for t in range(NT):
            quad = open_quad(*[orb_t[t, a // 3, (a % 3) * 3 + k] for k in range(3)])
            for b in range(4):
                orb_u[t, plane(4 * a + b), :] = quad[b]
        return 0

    lax.fori_loop(0, QUADS, open_orb, 0, unroll=2)
    for t in range(NT):
        sum_c(0, t)
        sum_d(0, t)

    def open_blk(t):
        def step(a, _):
            quad = open_quad(*[full[0, t, a // 3, (a % 3) * 3 + k] for k in range(3)])
            for b in range(4):
                blk_u[t, plane(4 * a + b), :] = quad[b]
            return 0

        lax.fori_loop(0, QUADS, step, 0, unroll=4)

    def transform_y(p0, p1):
        vh, vl = split(jnp.concatenate([p0, p1], axis=1))
        out = dot(left_y[...], jnp.concatenate([vh, vl], axis=0))
        out = out[:NG] + out[NG:]
        return out[:, :128], out[:, 128:]

    def transform_z(value):
        vh, vl = split(value)
        out = dot(jnp.concatenate([vh, vl], axis=1), right_z[...])
        return out[:, :128] + out[:, 128:]

    def forward(j, t):
        def rows(s, _):
            blk = blk_u[t, across(2 * s + j), :]
            out0, out1 = transform_y(
                orb_u[t, across(2 * s), :] * blk, orb_u[t, across(2 * s + 1), :] * blk
            )
            turned[across(2 * s), :] = out0
            turned[across(2 * s + 1), :] = out1
            return 0

        lax.fori_loop(0, 4, rows, 0, unroll=2)

        def half(h, _):
            out = transform_z(turned[pl.ds(pl.multiple_of(384 * h, 8), 384), :])
            for g in range(4):
                for s in range(3):
                    base = 96 * g + 32 * s
                    tiles = close_quad(*[out[base + 8 * b : base + 8 * b + 8] for b in range(4)])
                    for k in range(3):
                        lane = 384 * s + 128 * k
                        send_a[j, t, 4 * h + g, :, lane : lane + 128] = tiles[k]
            return 0

        lax.fori_loop(0, 2, half, 0)
        for o in range(1, NF):
            copy_a(j, t, turn(o), me).start()
        recv_a[j, t, me] = send_a[j, t, me]

    def middle(j):
        for t in range(NT):
            for o in range(1, NF):
                copy_a(j, t, turn(o), turn(o)).wait_recv()

        def step(s, _):
            cols = pl.ds(pl.multiple_of(384 * s, 128), 384)
            value = recv_a[j, :, :, :, cols].reshape(NL * NG, 384)
            spectrum = left_product(left_fx[...], value)
            weight = coulomb[:, cols]
            scaled = jnp.concatenate([spectrum[:NG] * weight, spectrum[NG:] * weight], axis=0)
            back = left_product(left_bx[...], scaled)
            send_b[j, :, :, :, cols] = back.reshape(NT, NF, 8, 384)
            return 0

        lax.fori_loop(0, 3, step, 0)
        for t in range(NT):
            for o in range(1, NF):
                copy_b(j, t, turn(o), me).start()
            recv_b[j, t, me] = send_b[j, t, me]

    def backward(j, t):
        for o in range(1, NF):
            copy_b(j, t, turn(o), turn(o)).wait_recv()

        def half(h, _):
            planes = []
            for g in range(4):
                for s in range(3):
                    planes += open_quad(
                        *[
                            recv_b[j, t, 4 * h + g, :, 384 * s + 128 * k : 384 * s + 128 * k + 128]
                            for k in range(3)
                        ]
                    )
            out = transform_z(jnp.concatenate(planes, axis=0))
            turned[pl.ds(pl.multiple_of(384 * h, 8), 384), :] = out
            return 0

        lax.fori_loop(0, 2, half, 0)

        def rows(s, _):
            even, odd = across(2 * s), across(2 * s + 1)
            pot0, pot1 = transform_y(turned[even, :], turned[odd, :])
            blk = blk_u[t, across(2 * s + j), :]
            term0, term1 = blk * pot0, blk * pot1
            if j > 0:
                term0 = local_u[t, even, :] + term0
                term1 = local_u[t, odd, :] + term1
            local_u[t, even, :] = term0
            local_u[t, odd, :] = term1
            block_u[t, across(2 * s + j), :] = (
                orb_u[t, even, :] * pot0 + orb_u[t, odd, :] * pot1
            )
            return 0

        lax.fori_loop(0, 4, rows, 0, unroll=2)

    def close_block(t):
        def step(a, _):
            tiles = close_quad(*[block_u[t, plane(4 * a + b), :] for b in range(4)])
            for k in range(3):
                source[1, t, a // 3, (a % 3) * 3 + k] = tiles[k]
            return 0

        lax.fori_loop(0, QUADS, step, 0, unroll=4)

    def write(ref, t, column, tile):
        lanes = pl.ds(pl.multiple_of(column * 128, 128), 128)
        ref[4 * t : 4 * t + 4, :, lanes] = tile.reshape(4, NL, 128)

    def write_local(a, _):
        for t in range(NT):
            tiles = close_quad(*[local_u[t, plane(4 * a + b), :] for b in range(4)])
            for k in range(3):
                write(local_ref, t, 3 * a + k, tiles[k])
        return 0

    def write_block(t):
        def step(c, _):
            write(block_ref, t, c, full[1, t, c // 9, c % 9])
            return 0

        lax.fori_loop(0, LANES // 128, step, 0, unroll=4)

    for t in range(NT):
        sum_e(0, t)
        sum_f(0, t)
        open_blk(t)
        forward(0, t)
    for t in range(NT):
        forward(1, t)
    middle(0)
    middle(1)
    for t in range(NT):
        backward(0, t)
    for t in range(NT):
        backward(1, t)
        close_block(t)
        sum_a(1, t)
        sum_b(1, t)
    lax.fori_loop(0, QUADS, write_local, 0, unroll=2)
    for t in range(NT):
        sum_c(1, t)
        sum_d(1, t)
    for t in range(NT):
        sum_e(1, t)
    for t in range(NT):
        sum_f(1, t)
        write_block(t)
    for t in range(NT):
        for j in range(NL):
            for o in range(1, NF):
                copy_a(j, t, turn(o), me).wait_send()
                copy_b(j, t, turn(o), me).wait_send()
            to_pair(j, t).wait_send()
            to_y(j, t).wait_send()
            to_mate(j, t, z).wait_send()
            for o in range(1, NZ):
                scatter(j, t, turn_z(o), z).wait_send()
                spread(j, t, turn_z(o), z).wait_send()
                to_mate(j, t, turn_z(o)).wait_send()


def per_device(orbitals, owners, cutoff_mask):
    vmem = pl.BlockSpec(memory_space=pltpu.VMEM)
    dma = pltpu.SemaphoreType.DMA

    def buffer(*shape):
        return pltpu.VMEM(shape, F32)

    planes = buffer(NT, PLANES, 128)
    tiles = buffer(2, NT, NZ, 9, 8, 128)
    pieces = buffer(2, NT, NZ, PART, 8, 128)
    single = buffer(2, NT, PART, 8, 128)
    grid = buffer(NL, NT, NF, 8, CHUNK)
    constants = [jnp.asarray(t) for t in tables()]
    flat = jax.ShapeDtypeStruct((NX, NL, LANES), F32)
    many = dma((2, NT, NF))
    few = dma((2, NT))
    local, block = pl.pallas_call(
        kernel,
        out_shape=(flat, flat),
        in_specs=[vmem, pl.BlockSpec(memory_space=pltpu.SMEM)] + [vmem] * (1 + len(constants)),
        out_specs=(vmem, vmem),
        scratch_shapes=[
            buffer(NG, CHUNK), buffer(NT, NZ, 9, 8, 128), tiles, tiles, planes, planes,
            buffer(PLANES, 128), planes, planes, grid, grid, grid, grid,
            pieces, pieces, pieces, single, single, pieces, pieces,
            many, many, many, many, few, few, few, few, many, many, many, many, many, many,
        ],
        compiler_params=pltpu.CompilerParams(
            collective_id=0, has_side_effects=True, vmem_limit_bytes=60 << 20
        ),
    )(orbitals.transpose(1, 0, 2), owners, cutoff_mask, *constants)
    return local.transpose(1, 0, 2), block.transpose(1, 0, 2)


def solution(mesh):
    in_specs = (P("band", "fft", None), P(), P(None, "fft"))
    out_specs = (P("band", "fft", None), P(None, "fft", None))
    return jax.shard_map(
        per_device, mesh=mesh, in_specs=in_specs, out_specs=out_specs, check_vma=False
    )
```

```python
import math

import jax
import jax.numpy as jnp
import numpy as np
from jax import lax
from jax.experimental import pallas as pl
from jax.experimental.pallas import tpu as pltpu
from jax.sharding import PartitionSpec as P

COULOMB = 400.0
EXCHANGE_MIX = 0.25
NG = 96
NL = 2
NX = 12
NF = 8
NZ = 8
NT = 3
LANES = NG * NG
CHUNK = NX * NG
QUADS = NG // 4
PLANES = NG * 8
PART = 5
MESH = pl.DeviceIdType.MESH
F32 = jnp.float32
BF16 = jnp.bfloat16
FAR = (4, 3, 5, 2, 6, 1, 7)
NEAR = (1, 7, 2, 6, 3, 5, 4)


def split_const(matrix):
    high = matrix.astype(np.float32).astype(jnp.bfloat16)
    low = (matrix.astype(np.float64) - np.asarray(high, np.float64)).astype(jnp.bfloat16)
    return np.asarray(high), np.asarray(low)


def tables():
    index = np.arange(NG)
    angle = 2.0 * math.pi * (index[:, None] * index[None, :] % NG) / NG
    cas = np.cos(angle) + np.sin(angle)
    cas_h, cas_l = split_const(cas)
    zero = np.zeros_like(cas_h)
    left_y = np.concatenate(
        [np.concatenate([cas_h, cas_h], 1), np.concatenate([cas_l, zero], 1)], 0
    )
    right_z = np.zeros((256, 256), cas_h.dtype)
    right_z[:NG, :NG] = cas_h
    right_z[128 : 128 + NG, :NG] = cas_h
    right_z[:NG, 128 : 128 + NG] = cas_l
    both = np.zeros((NL, NG, NT, NF, 4, NL))
    for i in range(NL):
        both[i, :, :, :, :, i] = cas.reshape(NG, NF, NT, 4).transpose(0, 2, 1, 3)
    both = both.reshape(NL * NG, NL * NG)
    left_fx = np.concatenate(split_const(both), 0)
    left_bx = np.concatenate(split_const(both.T), 0)
    signed = np.where(index <= NG // 2, index, index - NG)
    lane_y = np.tile(np.repeat(np.arange(NX), NG)[None], (8, 1)).astype(np.int32)
    lane_z = np.tile(np.tile(signed * signed, NX)[None], (8, 1)).astype(np.int32)
    row_x = np.tile((signed * signed)[:, None], (1, 128)).astype(np.int32)
    return [left_y, right_z, left_fx, left_bx, lane_y, lane_z, row_x]


def dot(a, b):
    return lax.dot_general(a, b, (((1,), (0,)), ((), ())), preferred_element_type=F32)


def split(value):
    high = value.astype(BF16)
    low = (value - high.astype(F32)).astype(BF16)
    return high, low


def left_product(left, value):
    rows = left.shape[0] // 2
    vh, vl = split(value)
    first = dot(left, vh)
    return first[:rows] + first[rows:] + dot(left[:rows], vl)


def open_quad(c0, c1, c2):
    lane = lax.broadcasted_iota(jnp.int32, c0.shape, 1)
    y1 = jnp.where(lane < 32, pltpu.roll(c0, 32, 1), pltpu.roll(c1, 32, 1))
    y2 = jnp.where(lane < 64, pltpu.roll(c1, 64, 1), pltpu.roll(c2, 64, 1))
    return c0, y1, y2, pltpu.roll(c2, 96, 1)


def close_quad(e0, e1, e2, e3):
    lane = lax.broadcasted_iota(jnp.int32, e0.shape, 1)
    r1 = pltpu.roll(e1, 96, 1)
    r2 = pltpu.roll(e2, 64, 1)
    r3 = pltpu.roll(e3, 32, 1)
    c0 = jnp.where(lane < 96, e0, r1)
    c1 = jnp.where(lane < 64, r1, r2)
    c2 = jnp.where(lane < 32, r2, r3)
    return c0, c1, c2


def plane(y):
    return pl.ds(pl.multiple_of(y * 8, 8), 8)


def across(row):
    return pl.ds(row, NG, stride=8)


def kernel(
    orb_hbm, owner_ref, mask_hbm, left_y_hbm, right_z_hbm, left_fx_hbm, left_bx_hbm,
    lane_y_hbm, lane_z_hbm, row_x_hbm, local_hbm, block_hbm,
    orb_ref, mask_ref, left_y, right_z, left_fx, left_bx, lane_y, lane_z, row_x,
    local_ref, block_ref, in_sem, out_sem,
    coulomb, source, full, orb_u, blk_u, turned, local_u, block_u,
    send_a, recv_a, send_b, recv_b, pair, part, gathered, summed, other, total, mate,
    sa_sem, ra_sem, sb_sem, rb_sem, ps_sem, pr_sem, ys_sem, yr_sem,
    zs_sem, zr_sem, gs_sem, gr_sem, ms_sem, mr_sem,
):
    me = lax.axis_index("fft")
    band = lax.axis_index("band")
    core = lax.rem(band, 2)
    z = lax.rem(band // 2, NZ)
    yh = band // (2 * NZ)
    mate_band = band + 1 - 2 * core
    y_band = lax.rem(band + 2 * NZ, 4 * NZ)

    def z_band(other_z):
        return (yh * NZ + other_z) * 2 + core

    def turn(o):
        return lax.rem(me + o, NF)

    def turn_z(o):
        return lax.rem(z + o, NZ)

    inputs = (
        (orb_hbm, orb_ref), (mask_hbm, mask_ref), (left_y_hbm, left_y), (right_z_hbm, right_z),
        (left_fx_hbm, left_fx), (left_bx_hbm, left_bx), (lane_y_hbm, lane_y),
        (lane_z_hbm, lane_z), (row_x_hbm, row_x),
    )
    fetches = [
        pltpu.make_async_copy(src, dst, in_sem.at[n]) for n, (src, dst) in enumerate(inputs)
    ]
    for fetch in fetches:
        fetch.start()
    barrier = pltpu.get_barrier_semaphore()
    devices = [{"fft": turn(o)} for o in range(1, NF)]
    devices += [{"band": mate_band}, {"band": y_band}]
    devices += [{"band": z_band(turn_z(o))} for o in range(1, NZ)]
    for device in devices:
        pl.semaphore_signal(barrier, inc=1, device_id=device, device_id_type=MESH)

    def remote(src, dst, send, recv, device):
        return pltpu.make_async_remote_copy(
            src_ref=src, dst_ref=dst, send_sem=send, recv_sem=recv,
            device_id=device, device_id_type=MESH,
        )

    def copy_a(j, t, peer, slot):
        return remote(
            send_a.at[j, t, peer], recv_a.at[j, t, slot],
            sa_sem.at[j, t, peer], ra_sem.at[j, t, slot], {"fft": peer},
        )

    def copy_b(j, t, peer, slot):
        return remote(
            send_b.at[j, t, peer], recv_b.at[j, t, slot],
            sb_sem.at[j, t, peer], rb_sem.at[j, t, slot], {"fft": peer},
        )

    def to_pair(q, j, t):
        return remote(
            source.at[q, j, t, :, pl.ds(4 * (1 - core), PART)], pair.at[q, j, t],
            ps_sem.at[q, j, t], pr_sem.at[q, j, t], {"band": mate_band},
        )

    def scatter(q, j, t, peer, slot):
        return remote(
            part.at[q, j, t, peer], gathered.at[q, j, t, slot],
            zs_sem.at[q, j, t, peer], zr_sem.at[q, j, t, slot], {"band": z_band(peer)},
        )

    def to_y(q, j, t):
        return remote(
            summed.at[q, j, t], other.at[q, j, t],
            ys_sem.at[q, j, t], yr_sem.at[q, j, t], {"band": y_band},
        )

    def spread(q, j, t, peer, slot):
        return remote(
            total.at[q, j, t, slot], total.at[q, j, t, slot],
            gs_sem.at[q, j, t, peer], gr_sem.at[q, j, t, slot], {"band": z_band(peer)},
        )

    def to_mate(q, j, t, slot):
        return remote(
            total.at[q, j, t, slot], mate.at[q, j, t, slot],
            ms_sem.at[q, j, t, slot], mr_sem.at[q, j, t, slot], {"band": mate_band},
        )

    def sum_a(q, j, t):
        to_pair(q, j, t).start()

    def sum_b(q, j, t):
        to_pair(q, j, t).wait_recv()

        def step(k, _):
            part[q, j, t, k] = source[q, j, t, k, pl.ds(4 * core, PART)] + pair[q, j, t, k]
            return 0

        lax.fori_loop(0, NZ, step, 0, unroll=2)
        for o in FAR:
            scatter(q, j, t, turn_z(o), z).start()
        gathered[q, j, t, z] = part[q, j, t, z]

    def sum_c(q, j, t):
        for o in FAR:
            scatter(q, j, t, turn_z(o), turn_z(o)).wait_recv()
        value = gathered[q, j, t, 0]
        for k in range(1, NZ):
            value = value + gathered[q, j, t, k]
        summed[q, j, t] = value
        to_y(q, j, t).start()

    def sum_d(q, j, t):
        to_y(q, j, t).wait_recv()
        total[q, j, t, z] = summed[q, j, t] + other[q, j, t]
        for o in FAR:
            spread(q, j, t, turn_z(o), z).start()
        to_mate(q, j, t, z).start()

    def sum_e(q, j, t):
        for o in NEAR:
            spread(q, j, t, turn_z(o), turn_z(o)).wait_recv()
            to_mate(q, j, t, turn_z(o)).start()

    def sum_f(q, j, t):
        for o in (0,) + NEAR:
            to_mate(q, j, t, turn_z(o)).wait_recv()

        def step(k, _):
            full[q, j, t, k, pl.ds(4 * core, PART)] = total[q, j, t, k]
            full[q, j, t, k, pl.ds(4 * (1 - core), PART)] = mate[q, j, t, k]
            return 0

        lax.fori_loop(0, NZ, step, 0, unroll=2)

    mine = jnp.broadcast_to(owner_ref[0], (4, 128)) == band

    def load_tiles(c, _):
        lanes = pl.ds(pl.multiple_of(c * 128, 128), 128)
        for t in range(NT):
            tile = orb_ref[4 * t : 4 * t + 4, :, lanes]
            for j in range(NL):
                source[0, j, t, c // 9, c % 9] = jnp.where(mine, tile[:, j, :], 0.0)
        return 0

    fetches[0].wait()
    lax.fori_loop(0, LANES // 128, load_tiles, 0, unroll=4)
    pl.semaphore_wait(barrier, len(devices))
    for j in range(NL):
        for t in range(NT):
            sum_a(0, j, t)
    for t in range(NT):
        sum_b(0, 0, t)
    sum_b(0, 1, 0)
    for fetch in fetches[1:]:
        fetch.wait()

    low = me * NX + lane_y[...]
    low = jnp.where(low <= NG // 2, low, low - NG)
    flat = low * low + lane_z[...]

    def coulomb_rows(k, _):
        rows = pl.ds(pl.multiple_of(8 * k, 8), 8)
        squared = jnp.concatenate([row_x[rows, :]] * 9, axis=1) + flat
        weight = mask_ref[rows, :].astype(F32)
        scale = -EXCHANGE_MIX * COULOMB / float(NG**3)
        coulomb[rows, :] = scale * weight / jnp.maximum(squared, 1).astype(F32)
        return 0

    lax.fori_loop(0, NG // 8, coulomb_rows, 0)

    def open_orb(a, _):
        for t in range(NT):
            tiles = []
            for k in range(3):
                lanes = pl.ds(pl.multiple_of(a * 384 + 128 * k, 128), 128)
                tiles.append(orb_ref[4 * t : 4 * t + 4, :, lanes].reshape(8, 128))
            quad = open_quad(*tiles)
            for b in range(4):
                orb_u[t, plane(4 * a + b), :] = quad[b]
        return 0

    lax.fori_loop(0, QUADS, open_orb, 0, unroll=2)

    def half_plane(y, j):
        return pl.ds(y * 8 + 4 * j, 4)

    def open_blk(j, t):
        def step(a, _):
            quad = open_quad(*[full[0, j, t, a // 3, (a % 3) * 3 + k] for k in range(3)])
            for b in range(4):
                blk_u[t, half_plane(4 * a + b, j), :] = quad[b]
            return 0

        lax.fori_loop(0, QUADS, step, 0, unroll=4)

    def transform_y(p0, p1):
        vh, vl = split(jnp.concatenate([p0, p1], axis=1))
        out = dot(left_y[...], jnp.concatenate([vh, vl], axis=0))
        out = out[:NG] + out[NG:]
        return out[:, :128], out[:, 128:]

    def transform_z(value):
        vh, vl = split(value)
        out = dot(jnp.concatenate([vh, vl], axis=1), right_z[...])
        return out[:, :128] + out[:, 128:]

    def forward(j, t):
        def rows(s, _):
            blk = blk_u[t, across(4 * j + s), :]
            out0, out1 = transform_y(
                orb_u[t, across(2 * s), :] * blk, orb_u[t, across(2 * s + 1), :] * blk
            )
            turned[across(2 * s), :] = out0
            turned[across(2 * s + 1), :] = out1
            return 0

        lax.fori_loop(0, 4, rows, 0, unroll=2)

        def half(h, _):
            out = transform_z(turned[pl.ds(pl.multiple_of(384 * h, 8), 384), :])
            for g in range(4):
                for s in range(3):
                    base = 96 * g + 32 * s
                    tiles = close_quad(*[out[base + 8 * b : base + 8 * b + 8] for b in range(4)])
                    for k in range(3):
                        lane = 384 * s + 128 * k
                        send_a[j, t, 4 * h + g, :, lane : lane + 128] = tiles[k]
            return 0

        lax.fori_loop(0, 2, half, 0)
        for o in range(1, NF):
            copy_a(j, t, turn(o), me).start()
        recv_a[j, t, me] = send_a[j, t, me]

    def middle(j):
        for t in range(NT):
            for o in range(1, NF):
                copy_a(j, t, turn(o), turn(o)).wait_recv()

        def step(s, _):
            cols = pl.ds(pl.multiple_of(384 * s, 128), 384)
            value = recv_a[j, :, :, :, cols].reshape(NL * NG, 384)
            spectrum = left_product(left_fx[...], value)
            weight = coulomb[:, cols]
            scaled = jnp.concatenate([spectrum[:NG] * weight, spectrum[NG:] * weight], axis=0)
            back = left_product(left_bx[...], scaled)
            send_b[j, :, :, :, cols] = back.reshape(NT, NF, 8, 384)
            return 0

        lax.fori_loop(0, 3, step, 0)
        for t in range(NT):
            for o in range(1, NF):
                copy_b(j, t, turn(o), me).start()
            recv_b[j, t, me] = send_b[j, t, me]

    def backward(j, t):
        for o in range(1, NF):
            copy_b(j, t, turn(o), turn(o)).wait_recv()

        def half(h, _):
            planes = []
            for g in range(4):
                for s in range(3):
                    planes += open_quad(
                        *[
                            recv_b[j, t, 4 * h + g, :, 384 * s + 128 * k : 384 * s + 128 * k + 128]
                            for k in range(3)
                        ]
                    )
            out = transform_z(jnp.concatenate(planes, axis=0))
            turned[pl.ds(pl.multiple_of(384 * h, 8), 384), :] = out
            return 0

        lax.fori_loop(0, 2, half, 0)

        def rows(s, _):
            even, odd = across(2 * s), across(2 * s + 1)
            pot0, pot1 = transform_y(turned[even, :], turned[odd, :])
            blk = blk_u[t, across(4 * j + s), :]
            term0, term1 = blk * pot0, blk * pot1
            if j > 0:
                term0 = local_u[t, even, :] + term0
                term1 = local_u[t, odd, :] + term1
            local_u[t, even, :] = term0
            local_u[t, odd, :] = term1
            block_u[t, across(4 * j + s), :] = (
                orb_u[t, even, :] * pot0 + orb_u[t, odd, :] * pot1
            )
            return 0

        lax.fori_loop(0, 4, rows, 0, unroll=2)

    def close_block(j, t):
        def step(a, _):
            tiles = close_quad(*[block_u[t, half_plane(4 * a + b, j), :] for b in range(4)])
            for k in range(3):
                source[1, j, t, a // 3, (a % 3) * 3 + k] = tiles[k]
            return 0

        lax.fori_loop(0, QUADS, step, 0, unroll=4)

    def write_local(a, _):
        for t in range(NT):
            tiles = close_quad(*[local_u[t, plane(4 * a + b), :] for b in range(4)])
            for k in range(3):
                lanes = pl.ds(pl.multiple_of(a * 384 + 128 * k, 128), 128)
                local_ref[4 * t : 4 * t + 4, :, lanes] = tiles[k].reshape(4, NL, 128)
        return 0

    def write_block(j, t):
        def step(c, _):
            lanes = pl.ds(pl.multiple_of(c * 128, 128), 128)
            block_ref[4 * t : 4 * t + 4, j, lanes] = full[1, j, t, c // 9, c % 9]
            return 0

        lax.fori_loop(0, LANES // 128, step, 0, unroll=4)

    def receive(j, t):
        sum_e(0, j, t)
        sum_f(0, j, t)
        open_blk(j, t)
        forward(j, t)

    def finish(j, t):
        sum_e(1, j, t)
        sum_f(1, j, t)
        write_block(j, t)

    def block_out(t):
        return pltpu.make_async_copy(
            block_ref.at[pl.ds(4 * t, 4)], block_hbm.at[pl.ds(4 * t, 4)], out_sem.at[t]
        )

    sum_c(0, 0, 0)
    sum_c(0, 0, 1)
    sum_c(0, 0, 2)
    sum_d(0, 0, 0)
    sum_b(0, 1, 1)
    sum_c(0, 1, 0)
    sum_d(0, 0, 1)
    sum_b(0, 1, 2)
    sum_d(0, 0, 2)
    sum_d(0, 1, 0)
    receive(0, 0)
    sum_c(0, 1, 1)
    receive(0, 1)
    sum_d(0, 1, 1)
    sum_c(0, 1, 2)
    receive(0, 2)
    sum_d(0, 1, 2)
    receive(1, 0)
    receive(1, 1)
    receive(1, 2)
    middle(0)
    middle(1)

    def back(j, t):
        backward(j, t)
        close_block(j, t)
        sum_a(1, j, t)

    back(0, 0)
    sum_b(1, 0, 0)
    back(0, 1)
    sum_b(1, 0, 1)
    back(0, 2)
    sum_b(1, 0, 2)
    sum_c(1, 0, 0)
    back(1, 0)
    sum_b(1, 1, 0)
    sum_c(1, 0, 1)
    sum_d(1, 0, 0)
    back(1, 1)
    sum_b(1, 1, 1)
    sum_c(1, 0, 2)
    sum_d(1, 0, 1)
    back(1, 2)
    sum_c(1, 1, 0)
    sum_d(1, 0, 2)
    sum_b(1, 1, 2)
    lax.fori_loop(0, QUADS, write_local, 0, unroll=2)
    local_out = pltpu.make_async_copy(local_ref, local_hbm, out_sem.at[NT])
    local_out.start()
    sum_c(1, 1, 1)
    sum_d(1, 1, 0)
    finish(0, 0)
    sum_d(1, 1, 1)
    finish(0, 1)
    sum_c(1, 1, 2)
    finish(0, 2)
    sum_d(1, 1, 2)
    for t in range(NT):
        finish(1, t)
        block_out(t).start()
    for t in range(NT):
        for j in range(NL):
            for o in range(1, NF):
                copy_a(j, t, turn(o), me).wait_send()
                copy_b(j, t, turn(o), me).wait_send()
            for q in range(2):
                to_pair(q, j, t).wait_send()
                to_y(q, j, t).wait_send()
                to_mate(q, j, t, z).wait_send()
                for o in range(1, NZ):
                    scatter(q, j, t, turn_z(o), z).wait_send()
                    spread(q, j, t, turn_z(o), z).wait_send()
                    to_mate(q, j, t, turn_z(o)).wait_send()
    local_out.wait()
    for t in range(NT):
        block_out(t).wait()


def per_device(orbitals, owners, cutoff_mask):
    dma = pltpu.SemaphoreType.DMA

    def buffer(*shape):
        return pltpu.VMEM(shape, F32)

    def like(array):
        return pltpu.VMEM(array.shape, array.dtype)

    planes = buffer(NT, PLANES, 128)
    tiles = buffer(2, NL, NT, NZ, 9, 4, 128)
    pieces = buffer(2, NL, NT, NZ, PART, 4, 128)
    single = buffer(2, NL, NT, PART, 4, 128)
    grid = buffer(NL, NT, NF, 8, CHUNK)
    constants = [jnp.asarray(t) for t in tables()]
    flat = jax.ShapeDtypeStruct((NX, NL, LANES), F32)
    many = dma((NL, NT, NF))
    bulk = dma((2, NL, NT, NZ))
    few = dma((2, NL, NT))
    anywhere = pl.BlockSpec(memory_space=pl.ANY)
    orb = orbitals.transpose(1, 0, 2)
    local, block = pl.pallas_call(
        kernel,
        out_shape=(flat, flat),
        in_specs=[anywhere, pl.BlockSpec(memory_space=pltpu.SMEM)]
        + [anywhere] * (1 + len(constants)),
        out_specs=(anywhere, anywhere),
        scratch_shapes=[
            like(orb), like(cutoff_mask), *[like(c) for c in constants],
            like(flat), like(flat), dma((2 + len(constants),)), dma((NT + 1,)),
            buffer(NG, CHUNK), tiles, tiles, planes, planes,
            buffer(PLANES, 128), planes, planes, grid, grid, grid, grid,
            pieces, pieces, pieces, single, single, pieces, pieces,
            many, many, many, many, few, few, few, few, bulk, bulk, bulk, bulk, bulk, bulk,
        ],
        compiler_params=pltpu.CompilerParams(
            collective_id=0, has_side_effects=True, vmem_limit_bytes=60 << 20
        ),
    )(orb, owners, cutoff_mask, *constants)
    return local.transpose(1, 0, 2), block.transpose(1, 0, 2)


def solution(mesh):
    in_specs = (P("band", "fft", None), P(), P(None, "fft"))
    out_specs = (P("band", "fft", None), P(None, "fft", None))
    return jax.shard_map(
        per_device, mesh=mesh, in_specs=in_specs, out_specs=out_specs, check_vma=False
    )
```

```python
import math

import jax
import jax.numpy as jnp
import numpy as np
from jax import lax
from jax.experimental import pallas as pl
from jax.experimental.pallas import tpu as pltpu
from jax.sharding import PartitionSpec as P

COULOMB = 400.0
EXCHANGE_MIX = 0.25
NG = 96
NL = 2
NX = 12
NF = 8
NZ = 8
NT = 3
LANES = NG * NG
CHUNK = NX * NG
QUADS = NG // 4
PLANES = NG * 8
PART = 5
MESH = pl.DeviceIdType.MESH
F32 = jnp.float32
BF16 = jnp.bfloat16
FAR = (4, 3, 5, 2, 6, 1, 7)


def split_const(matrix):
    high = matrix.astype(np.float32).astype(jnp.bfloat16)
    low = (matrix.astype(np.float64) - np.asarray(high, np.float64)).astype(jnp.bfloat16)
    return np.asarray(high), np.asarray(low)


def tables():
    index = np.arange(NG)
    angle = 2.0 * math.pi * (index[:, None] * index[None, :] % NG) / NG
    cas = np.cos(angle) + np.sin(angle)
    cas_h, cas_l = split_const(cas)
    zero = np.zeros_like(cas_h)
    left_y = np.concatenate(
        [np.concatenate([cas_h, cas_h], 1), np.concatenate([cas_l, zero], 1)], 0
    )
    right_z = np.zeros((256, 256), cas_h.dtype)
    right_z[:NG, :NG] = cas_h
    right_z[128 : 128 + NG, :NG] = cas_h
    right_z[:NG, 128 : 128 + NG] = cas_l
    both = np.zeros((NL, NG, NT, NF, 4, NL))
    for i in range(NL):
        both[i, :, :, :, :, i] = cas.reshape(NG, NF, NT, 4).transpose(0, 2, 1, 3)
    both = both.reshape(NL * NG, NL * NG)
    left_fx = np.concatenate(split_const(both), 0)
    left_bx = np.concatenate(split_const(both.T), 0)
    packed = np.zeros((1216, 256), cas_h.dtype)
    packed[:192, :192] = left_y
    packed[192:448] = right_z
    packed[448:832, :192] = left_fx
    packed[832:1216, :192] = left_bx
    return packed


def dot(a, b):
    return lax.dot_general(a, b, (((1,), (0,)), ((), ())), preferred_element_type=F32)


def split(value):
    high = value.astype(BF16)
    low = (value - high.astype(F32)).astype(BF16)
    return high, low


def left_product(left, value):
    rows = left.shape[0] // 2
    vh, vl = split(value)
    first = dot(left, vh)
    return first[:rows] + first[rows:] + dot(left[:rows], vl)


def open_quad(c0, c1, c2):
    lane = lax.broadcasted_iota(jnp.int32, c0.shape, 1)
    y1 = jnp.where(lane < 32, pltpu.roll(c0, 32, 1), pltpu.roll(c1, 32, 1))
    y2 = jnp.where(lane < 64, pltpu.roll(c1, 64, 1), pltpu.roll(c2, 64, 1))
    return c0, y1, y2, pltpu.roll(c2, 96, 1)


def close_quad(e0, e1, e2, e3):
    lane = lax.broadcasted_iota(jnp.int32, e0.shape, 1)
    r1 = pltpu.roll(e1, 96, 1)
    r2 = pltpu.roll(e2, 64, 1)
    r3 = pltpu.roll(e3, 32, 1)
    c0 = jnp.where(lane < 96, e0, r1)
    c1 = jnp.where(lane < 64, r1, r2)
    c2 = jnp.where(lane < 32, r2, r3)
    return c0, c1, c2


def plane(y):
    return pl.ds(pl.multiple_of(y * 8, 8), 8)


def across(row):
    return pl.ds(row, NG, stride=8)


def kernel(
    orb_hbm, owner_ref, mask_hbm, weights_hbm, local_hbm, block_hbm,
    orb_ref, mask_ref, weights,
    local_ref, block_ref, in_sem, out_sem,
    coulomb, source, full, orb_u, blk_u, turned, local_u, block_u,
    send_a, recv_a, send_b, recv_b, pair, part, gathered, summed, other, total, mate,
    sa_sem, ra_sem, sb_sem, rb_sem, ps_sem, pr_sem, ys_sem, yr_sem,
    zs_sem, zr_sem, gs_sem, gr_sem, ms_sem, mr_sem,
):
    me = lax.axis_index("fft")
    band = lax.axis_index("band")
    core = lax.rem(band, 2)
    z = lax.rem(band // 2, NZ)
    yh = band // (2 * NZ)
    mate_band = band + 1 - 2 * core
    y_band = lax.rem(band + 2 * NZ, 4 * NZ)

    def z_band(other_z):
        return (yh * NZ + other_z) * 2 + core

    def turn(o):
        return lax.rem(me + o, NF)

    def turn_z(o):
        return lax.rem(z + o, NZ)

    inputs = (
        (orb_hbm, orb_ref), (mask_hbm, mask_ref), (weights_hbm, weights),
    )
    fetches = [
        pltpu.make_async_copy(src, dst, in_sem.at[n]) for n, (src, dst) in enumerate(inputs)
    ]
    for fetch in fetches:
        fetch.start()
    barrier = pltpu.get_barrier_semaphore()
    devices = [{"fft": turn(o)} for o in range(1, NF)]
    devices += [{"band": mate_band}, {"band": y_band}]
    devices += [{"band": z_band(turn_z(o))} for o in range(1, NZ)]
    for device in devices:
        pl.semaphore_signal(barrier, inc=1, device_id=device, device_id_type=MESH)

    def remote(src, dst, send, recv, device):
        return pltpu.make_async_remote_copy(
            src_ref=src, dst_ref=dst, send_sem=send, recv_sem=recv,
            device_id=device, device_id_type=MESH,
        )

    others = pl.ds(0, NF - 1)

    def copy_a(j, t, peer, slot):
        return remote(
            send_a.at[j, t, peer], recv_a.at[j, t, slot],
            sa_sem.at[j, t], ra_sem.at[j, t], {"fft": turn(1) if peer is others else peer},
        )

    def copy_b(j, t, peer, slot):
        return remote(
            send_b.at[j, t, peer], recv_b.at[j, t, slot],
            sb_sem.at[j, t], rb_sem.at[j, t], {"fft": turn(1) if peer is others else peer},
        )

    def to_pair(q, j, t):
        return remote(
            source.at[q, j, t, :, pl.ds(4 * (1 - core), PART)], pair.at[q, j, t],
            ps_sem.at[q, j, t], pr_sem.at[q, j, t], {"band": mate_band},
        )

    def scatter(q, j, t, peer, slot):
        return remote(
            part.at[q, j, t, peer], gathered.at[q, j, t, slot],
            zs_sem.at[q, j, t], zr_sem.at[q, j, t],
            {"band": z_band(turn_z(1) if peer is others else peer)},
        )

    def to_y(q, j, t):
        return remote(
            summed.at[q, j, t], other.at[q, j, t],
            ys_sem.at[q, j, t], yr_sem.at[q, j, t], {"band": y_band},
        )

    def spread(q, j, t, peer, slot):
        return remote(
            total.at[q, j, t, slot], total.at[q, j, t, slot],
            gs_sem.at[q, j, t], gr_sem.at[q, j, t],
            {"band": z_band(turn_z(1) if peer is others else peer)},
        )

    def to_mate(q, j, t):
        return remote(
            total.at[q, j, t], mate.at[q, j, t],
            ms_sem.at[q, j, t], mr_sem.at[q, j, t], {"band": mate_band},
        )

    def sum_a(q, j, t):
        to_pair(q, j, t).start()

    def sum_b(q, j, t):
        to_pair(q, j, t).wait_recv()

        def step(k, _):
            part[q, j, t, k] = source[q, j, t, k, pl.ds(4 * core, PART)] + pair[q, j, t, k]
            return 0

        lax.fori_loop(0, NZ, step, 0, unroll=2)
        for o in FAR:
            scatter(q, j, t, turn_z(o), z).start()
        gathered[q, j, t, z] = part[q, j, t, z]

    def sum_c(q, j, t):
        scatter(q, j, t, others, others).wait_recv()
        value = gathered[q, j, t, 0]
        for k in range(1, NZ):
            value = value + gathered[q, j, t, k]
        summed[q, j, t] = value
        to_y(q, j, t).start()

    def sum_d(q, j, t):
        to_y(q, j, t).wait_recv()
        total[q, j, t, z] = summed[q, j, t] + other[q, j, t]
        for o in FAR:
            spread(q, j, t, turn_z(o), z).start()

    def sum_e(q, j, t):
        spread(q, j, t, others, others).wait_recv()
        to_mate(q, j, t).start()

    def sum_f(q, j, t):
        to_mate(q, j, t).wait_recv()

        def step(k, _):
            full[q, j, t, k, pl.ds(4 * core, PART)] = total[q, j, t, k]
            full[q, j, t, k, pl.ds(4 * (1 - core), PART)] = mate[q, j, t, k]
            return 0

        lax.fori_loop(0, NZ, step, 0, unroll=2)

    mine = jnp.broadcast_to(owner_ref[0], (4, 128)) == band

    def load_tiles(c, _):
        lanes = pl.ds(pl.multiple_of(c * 128, 128), 128)
        for t in range(NT):
            tile = orb_ref[4 * t : 4 * t + 4, :, lanes]
            for j in range(NL):
                source[0, j, t, c // 9, c % 9] = jnp.where(mine, tile[:, j, :], 0.0)
        return 0

    fetches[0].wait()
    lax.fori_loop(0, LANES // 128, load_tiles, 0, unroll=4)
    pl.semaphore_wait(barrier, len(devices))
    for j in range(NL):
        for t in range(NT):
            sum_a(0, j, t)
    for t in range(NT):
        sum_b(0, 0, t)
    sum_b(0, 1, 0)
    for fetch in fetches[1:]:
        fetch.wait()

    def square(value):
        value = jnp.where(value <= NG // 2, value, value - NG)
        return value * value

    lane = lax.broadcasted_iota(jnp.int32, (8, CHUNK), 1)
    lane_y = (lane * 683) >> 16
    flat = square(me * NX + lane_y) + square(lane - NG * lane_y)
    row = lax.broadcasted_iota(jnp.int32, (8, CHUNK), 0)

    def coulomb_rows(k, _):
        rows = pl.ds(pl.multiple_of(8 * k, 8), 8)
        squared = square(8 * k + row) + flat
        weight = mask_ref[rows, :].astype(F32)
        scale = -EXCHANGE_MIX * COULOMB / float(NG**3)
        coulomb[rows, :] = scale * weight / jnp.maximum(squared, 1).astype(F32)
        return 0

    lax.fori_loop(0, NG // 8, coulomb_rows, 0)

    def open_orb(a, _):
        for t in range(NT):
            tiles = []
            for k in range(3):
                lanes = pl.ds(pl.multiple_of(a * 384 + 128 * k, 128), 128)
                tiles.append(orb_ref[4 * t : 4 * t + 4, :, lanes].reshape(8, 128))
            quad = open_quad(*tiles)
            for b in range(4):
                orb_u[t, plane(4 * a + b), :] = quad[b]
        return 0

    lax.fori_loop(0, QUADS, open_orb, 0, unroll=2)

    def half_plane(y, j):
        return pl.ds(y * 8 + 4 * j, 4)

    def open_blk(j, t):
        def step(a, _):
            quad = open_quad(*[full[0, j, t, a // 3, (a % 3) * 3 + k] for k in range(3)])
            for b in range(4):
                blk_u[t, half_plane(4 * a + b, j), :] = quad[b]
            return 0

        lax.fori_loop(0, QUADS, step, 0, unroll=4)

    def transform_y(p0, p1):
        vh, vl = split(jnp.concatenate([p0, p1], axis=1))
        out = dot(weights[:192, :192], jnp.concatenate([vh, vl], axis=0))
        out = out[:NG] + out[NG:]
        return out[:, :128], out[:, 128:]

    def transform_z(value):
        vh, vl = split(value)
        out = dot(jnp.concatenate([vh, vl], axis=1), weights[192:448, :])
        return out[:, :128] + out[:, 128:]

    def forward(j, t):
        def rows(s, _):
            blk = blk_u[t, across(4 * j + s), :]
            out0, out1 = transform_y(
                orb_u[t, across(2 * s), :] * blk, orb_u[t, across(2 * s + 1), :] * blk
            )
            turned[across(2 * s), :] = out0
            turned[across(2 * s + 1), :] = out1
            return 0

        lax.fori_loop(0, 4, rows, 0, unroll=2)

        def half(h, _):
            out = transform_z(turned[pl.ds(pl.multiple_of(384 * h, 8), 384), :])
            for g in range(4):
                for s in range(3):
                    base = 96 * g + 32 * s
                    tiles = close_quad(*[out[base + 8 * b : base + 8 * b + 8] for b in range(4)])
                    for k in range(3):
                        lane = 384 * s + 128 * k
                        send_a[j, t, 4 * h + g, :, lane : lane + 128] = tiles[k]
            return 0

        lax.fori_loop(0, 2, half, 0)
        for o in range(1, NF):
            copy_a(j, t, turn(o), me).start()
        recv_a[j, t, me] = send_a[j, t, me]

    def middle(j):
        for t in range(NT):
            copy_a(j, t, others, others).wait_recv()

        def step(s, _):
            cols = pl.ds(pl.multiple_of(384 * s, 128), 384)
            value = recv_a[j, :, :, :, cols].reshape(NL * NG, 384)
            spectrum = left_product(weights[448:832, :192], value)
            weight = coulomb[:, cols]
            scaled = jnp.concatenate([spectrum[:NG] * weight, spectrum[NG:] * weight], axis=0)
            back = left_product(weights[832:1216, :192], scaled)
            send_b[j, :, :, :, cols] = back.reshape(NT, NF, 8, 384)
            return 0

        lax.fori_loop(0, 3, step, 0)
        for t in range(NT):
            for o in range(1, NF):
                copy_b(j, t, turn(o), me).start()
            recv_b[j, t, me] = send_b[j, t, me]

    def backward(j, t):
        copy_b(j, t, others, others).wait_recv()

        def half(h, _):
            planes = []
            for g in range(4):
                for s in range(3):
                    planes += open_quad(
                        *[
                            recv_b[j, t, 4 * h + g, :, 384 * s + 128 * k : 384 * s + 128 * k + 128]
                            for k in range(3)
                        ]
                    )
            out = transform_z(jnp.concatenate(planes, axis=0))
            turned[pl.ds(pl.multiple_of(384 * h, 8), 384), :] = out
            return 0

        lax.fori_loop(0, 2, half, 0)

        def rows(s, _):
            even, odd = across(2 * s), across(2 * s + 1)
            pot0, pot1 = transform_y(turned[even, :], turned[odd, :])
            blk = blk_u[t, across(4 * j + s), :]
            term0, term1 = blk * pot0, blk * pot1
            if j > 0:
                term0 = local_u[t, even, :] + term0
                term1 = local_u[t, odd, :] + term1
            local_u[t, even, :] = term0
            local_u[t, odd, :] = term1
            block_u[t, across(4 * j + s), :] = (
                orb_u[t, even, :] * pot0 + orb_u[t, odd, :] * pot1
            )
            return 0

        lax.fori_loop(0, 4, rows, 0, unroll=2)

    def close_block(j, t):
        def step(a, _):
            tiles = close_quad(*[block_u[t, half_plane(4 * a + b, j), :] for b in range(4)])
            for k in range(3):
                source[1, j, t, a // 3, (a % 3) * 3 + k] = tiles[k]
            return 0

        lax.fori_loop(0, QUADS, step, 0, unroll=4)

    def write_local(a, _):
        for t in range(NT):
            tiles = close_quad(*[local_u[t, plane(4 * a + b), :] for b in range(4)])
            for k in range(3):
                lanes = pl.ds(pl.multiple_of(a * 384 + 128 * k, 128), 128)
                local_ref[4 * t : 4 * t + 4, :, lanes] = tiles[k].reshape(4, NL, 128)
        return 0

    def write_block(j, t):
        def step(c, _):
            lanes = pl.ds(pl.multiple_of(c * 128, 128), 128)
            block_ref[4 * t : 4 * t + 4, j, lanes] = full[1, j, t, c // 9, c % 9]
            return 0

        lax.fori_loop(0, LANES // 128, step, 0, unroll=4)

    def receive(j, t):
        sum_f(0, j, t)
        open_blk(j, t)
        forward(j, t)

    def finish(j, t):
        sum_f(1, j, t)
        write_block(j, t)

    def block_out(t):
        return pltpu.make_async_copy(
            block_ref.at[pl.ds(4 * t, 4)], block_hbm.at[pl.ds(4 * t, 4)], out_sem.at[t]
        )

    sum_c(0, 0, 0)
    sum_c(0, 0, 1)
    sum_c(0, 0, 2)
    sum_d(0, 0, 0)
    sum_b(0, 1, 1)
    sum_c(0, 1, 0)
    sum_d(0, 0, 1)
    sum_b(0, 1, 2)
    sum_d(0, 0, 2)
    sum_e(0, 0, 0)
    sum_d(0, 1, 0)
    receive(0, 0)
    sum_c(0, 1, 1)
    sum_e(0, 0, 1)
    sum_c(0, 1, 2)
    receive(0, 1)
    sum_d(0, 1, 1)
    sum_e(0, 0, 2)
    sum_d(0, 1, 2)
    receive(0, 2)
    sum_e(0, 1, 0)
    receive(1, 0)
    sum_e(0, 1, 1)
    receive(1, 1)
    sum_e(0, 1, 2)
    receive(1, 2)

    def sum_sent(q, j, t):
        to_pair(q, j, t).wait_send()
        to_y(q, j, t).wait_send()
        to_mate(q, j, t).wait_send()
        scatter(q, j, t, others, others).wait_send()
        spread(q, j, t, others, others).wait_send()

    middle(0)
    for j in range(NL):
        for t in range(NT):
            sum_sent(0, j, t)
    middle(1)

    def back(j, t):
        backward(j, t)
        close_block(j, t)
        sum_a(1, j, t)

    back(0, 0)
    back(0, 1)
    sum_b(1, 0, 0)
    back(0, 2)
    sum_b(1, 0, 1)
    back(1, 0)
    sum_b(1, 0, 2)
    sum_c(1, 0, 0)
    back(1, 1)
    sum_b(1, 1, 0)
    sum_c(1, 0, 1)
    back(1, 2)
    sum_b(1, 1, 1)
    sum_c(1, 0, 2)
    sum_d(1, 0, 0)
    lax.fori_loop(0, QUADS // 2, write_local, 0, unroll=2)
    sum_b(1, 1, 2)
    lax.fori_loop(QUADS // 2, QUADS, write_local, 0, unroll=2)
    local_out = pltpu.make_async_copy(local_ref, local_hbm, out_sem.at[NT])
    local_out.start()
    sum_d(1, 0, 1)
    sum_c(1, 1, 0)
    sum_d(1, 0, 2)
    sum_c(1, 1, 1)
    sum_d(1, 1, 0)
    sum_c(1, 1, 2)
    sum_d(1, 1, 1)
    sum_d(1, 1, 2)
    for t in range(NT):
        sum_e(1, 0, t)
    for t in range(NT):
        finish(0, t)
    for j in range(NL):
        for t in range(NT):
            copy_a(j, t, others, others).wait_send()
            copy_b(j, t, others, others).wait_send()
    for t in range(NT):
        sum_e(1, 1, t)
        if t > 0:
            finish(1, t - 1)
            block_out(t - 1).start()
    finish(1, NT - 1)
    block_out(NT - 1).start()
    for j in range(NL):
        for t in range(NT):
            sum_sent(1, j, t)
    local_out.wait()
    for t in range(NT):
        block_out(t).wait()


def per_device(orbitals, owners, cutoff_mask):
    dma = pltpu.SemaphoreType.DMA

    def buffer(*shape):
        return pltpu.VMEM(shape, F32)

    def like(array):
        return pltpu.VMEM(array.shape, array.dtype)

    planes = buffer(NT, PLANES, 128)
    tiles = buffer(2, NL, NT, NZ, 9, 4, 128)
    pieces = buffer(2, NL, NT, NZ, PART, 4, 128)
    single = buffer(2, NL, NT, PART, 4, 128)
    grid = buffer(NL, NT, NF, 8, CHUNK)
    constants = jnp.asarray(tables())
    flat = jax.ShapeDtypeStruct((NX, NL, LANES), F32)
    many = dma((NL, NT))
    few = dma((2, NL, NT))
    anywhere = pl.BlockSpec(memory_space=pl.ANY)
    stay = pl.BlockSpec(memory_space=pltpu.HBM)
    orb = orbitals.transpose(1, 0, 2)
    local, block = pl.pallas_call(
        kernel,
        out_shape=(flat, flat),
        in_specs=[stay, pl.BlockSpec(memory_space=pltpu.SMEM)]
        + [stay] * 2,
        out_specs=(anywhere, anywhere),
        scratch_shapes=[
            like(orb), like(cutoff_mask), like(constants),
            like(flat), like(flat), dma((3,)), dma((NT + 1,)),
            buffer(NG, CHUNK), tiles, tiles, planes, planes,
            buffer(PLANES, 128), planes, planes, grid, grid, grid, grid,
            pieces, pieces, pieces, single, single, pieces, pieces,
            many, many, many, many, few, few, few, few, few, few, few, few, few, few,
        ],
        compiler_params=pltpu.CompilerParams(
            collective_id=0, has_side_effects=True, vmem_limit_bytes=60 << 20
        ),
    )(orb, owners, cutoff_mask, constants)
    return local.transpose(1, 0, 2), block.transpose(1, 0, 2)


def solution(mesh):
    in_specs = (P("band", "fft", None), P(), P(None, "fft"))
    out_specs = (P("band", "fft", None), P(None, "fft", None))
    return jax.shard_map(
        per_device, mesh=mesh, in_specs=in_specs, out_specs=out_specs, check_vma=False
    )
```

```python
import math

import jax
import jax.numpy as jnp
import numpy as np
from jax import lax
from jax.experimental import pallas as pl
from jax.experimental.pallas import tpu as pltpu
from jax.sharding import PartitionSpec as P

COULOMB = 400.0
EXCHANGE_MIX = 0.25
NG = 96
NL = 2
NX = 12
NF = 8
NZ = 8
NT = 3
LANES = NG * NG
CHUNK = NX * NG
QUADS = NG // 4
PLANES = NG * 8
PART = 5
MESH = pl.DeviceIdType.MESH
F32 = jnp.float32
BF16 = jnp.bfloat16
FAR = (4, 3, 5, 2, 6, 1, 7)


def split_const(matrix):
    high = matrix.astype(np.float32).astype(jnp.bfloat16)
    low = (matrix.astype(np.float64) - np.asarray(high, np.float64)).astype(jnp.bfloat16)
    return np.asarray(high), np.asarray(low)


def tables():
    index = np.arange(NG)
    angle = 2.0 * math.pi * (index[:, None] * index[None, :] % NG) / NG
    cas = np.cos(angle) + np.sin(angle)
    cas_h, cas_l = split_const(cas)
    zero = np.zeros_like(cas_h)
    left_y = np.concatenate(
        [np.concatenate([cas_h, cas_h], 1), np.concatenate([cas_l, zero], 1)], 0
    )
    right_z = np.zeros((256, 256), cas_h.dtype)
    right_z[:NG, :NG] = cas_h
    right_z[128 : 128 + NG, :NG] = cas_h
    right_z[:NG, 128 : 128 + NG] = cas_l
    both = np.zeros((NL, NG, NT, NF, 4, NL))
    for i in range(NL):
        both[i, :, :, :, :, i] = cas.reshape(NG, NF, NT, 4).transpose(0, 2, 1, 3)
    both = both.reshape(NL * NG, NL * NG)
    left_fx = np.concatenate(split_const(both), 0)
    left_bx = np.concatenate(split_const(both.T), 0)
    packed = np.zeros((1216, 256), cas_h.dtype)
    packed[:192, :192] = left_y
    packed[192:448] = right_z
    packed[448:832, :192] = left_fx
    packed[832:1216, :192] = left_bx
    return packed


def dot(a, b):
    return lax.dot_general(a, b, (((1,), (0,)), ((), ())), preferred_element_type=F32)


def split(value):
    high = value.astype(BF16)
    low = (value - high.astype(F32)).astype(BF16)
    return high, low


def left_product(left, value):
    rows = left.shape[0] // 2
    vh, vl = split(value)
    first = dot(left, vh)
    return first[:rows] + first[rows:] + dot(left[:rows], vl)


def open_quad(c0, c1, c2):
    lane = lax.broadcasted_iota(jnp.int32, c0.shape, 1)
    y1 = jnp.where(lane < 32, pltpu.roll(c0, 32, 1), pltpu.roll(c1, 32, 1))
    y2 = jnp.where(lane < 64, pltpu.roll(c1, 64, 1), pltpu.roll(c2, 64, 1))
    return c0, y1, y2, pltpu.roll(c2, 96, 1)


def close_quad(e0, e1, e2, e3):
    lane = lax.broadcasted_iota(jnp.int32, e0.shape, 1)
    r1 = pltpu.roll(e1, 96, 1)
    r2 = pltpu.roll(e2, 64, 1)
    r3 = pltpu.roll(e3, 32, 1)
    c0 = jnp.where(lane < 96, e0, r1)
    c1 = jnp.where(lane < 64, r1, r2)
    c2 = jnp.where(lane < 32, r2, r3)
    return c0, c1, c2


def plane(y):
    return pl.ds(pl.multiple_of(y * 8, 8), 8)


def across(row):
    return pl.ds(row, NG, stride=8)


def kernel(
    orb_hbm, owner_ref, mask_hbm, weights_hbm, local_hbm, block_hbm,
    orb_ref, mask_ref, weights,
    local_ref, block_ref, in_sem, out_sem,
    coulomb, source, full, orb_u, blk_u, turned, local_u, block_u,
    send_a, recv_a, send_b, recv_b, pair, part, gathered, summed, other, total, mate,
    sa_sem, ra_sem, sb_sem, rb_sem, ps_sem, pr_sem, ys_sem, yr_sem,
    zs_sem, zr_sem, gs_sem, gr_sem, ms_sem, mr_sem,
):
    me = lax.axis_index("fft")
    band = lax.axis_index("band")
    core = lax.rem(band, 2)
    z = lax.rem(band // 2, NZ)
    yh = band // (2 * NZ)
    mate_band = band + 1 - 2 * core
    y_band = lax.rem(band + 2 * NZ, 4 * NZ)

    def z_band(other_z):
        return (yh * NZ + other_z) * 2 + core

    def turn(o):
        return lax.rem(me + o, NF)

    def turn_z(o):
        return lax.rem(z + o, NZ)

    fetches = []
    for t in range(NT):
        rows = pl.ds(4 * t, 4)
        fetches.append(
            pltpu.make_async_copy(orb_hbm.at[rows], orb_ref.at[rows], in_sem.at[t])
        )
    fetches.append(pltpu.make_async_copy(mask_hbm, mask_ref, in_sem.at[NT]))
    fetches.append(pltpu.make_async_copy(weights_hbm, weights, in_sem.at[NT + 1]))
    for fetch in fetches:
        fetch.start()
    barrier = pltpu.get_barrier_semaphore()
    devices = [{"fft": turn(o)} for o in range(1, NF)]
    devices += [{"band": mate_band}, {"band": y_band}]
    devices += [{"band": z_band(turn_z(o))} for o in range(1, NZ)]
    for device in devices:
        pl.semaphore_signal(barrier, inc=1, device_id=device, device_id_type=MESH)

    def remote(src, dst, send, recv, device):
        return pltpu.make_async_remote_copy(
            src_ref=src, dst_ref=dst, send_sem=send, recv_sem=recv,
            device_id=device, device_id_type=MESH,
        )

    others = pl.ds(0, NF - 1)

    def copy_a(j, t, peer, slot):
        return remote(
            send_a.at[j, t, peer], recv_a.at[j, t, slot],
            sa_sem.at[j, t], ra_sem.at[j, t], {"fft": turn(1) if peer is others else peer},
        )

    def copy_b(j, t, peer, slot):
        return remote(
            send_b.at[j, t, peer], recv_b.at[j, t, slot],
            sb_sem.at[j, t], rb_sem.at[j, t], {"fft": turn(1) if peer is others else peer},
        )

    def to_pair(q, j, t):
        return remote(
            source.at[q, j, t, :, pl.ds(4 * (1 - core), PART)], pair.at[q, j, t],
            ps_sem.at[q, j, t], pr_sem.at[q, j, t], {"band": mate_band},
        )

    def scatter(q, j, t, peer, slot):
        return remote(
            part.at[q, j, t, peer], gathered.at[q, j, t, slot],
            zs_sem.at[q, j, t], zr_sem.at[q, j, t],
            {"band": z_band(turn_z(1) if peer is others else peer)},
        )

    def to_y(q, j, t):
        return remote(
            summed.at[q, j, t], other.at[q, j, t],
            ys_sem.at[q, j, t], yr_sem.at[q, j, t], {"band": y_band},
        )

    def spread(q, j, t, peer, slot):
        return remote(
            total.at[q, j, t, slot], total.at[q, j, t, slot],
            gs_sem.at[q, j, t], gr_sem.at[q, j, t],
            {"band": z_band(turn_z(1) if peer is others else peer)},
        )

    def to_mate(q, j, t):
        return remote(
            total.at[q, j, t], mate.at[q, j, t],
            ms_sem.at[q, j, t], mr_sem.at[q, j, t], {"band": mate_band},
        )

    def sum_a(q, j, t):
        to_pair(q, j, t).start()

    def sum_b(q, j, t):
        to_pair(q, j, t).wait_recv()

        def step(k, _):
            part[q, j, t, k] = source[q, j, t, k, pl.ds(4 * core, PART)] + pair[q, j, t, k]
            return 0

        lax.fori_loop(0, NZ, step, 0, unroll=2)
        for o in FAR:
            scatter(q, j, t, turn_z(o), z).start()
        gathered[q, j, t, z] = part[q, j, t, z]

    def sum_c(q, j, t):
        scatter(q, j, t, others, others).wait_recv()
        value = gathered[q, j, t, 0]
        for k in range(1, NZ):
            value = value + gathered[q, j, t, k]
        summed[q, j, t] = value
        to_y(q, j, t).start()

    def sum_d(q, j, t):
        to_y(q, j, t).wait_recv()
        total[q, j, t, z] = summed[q, j, t] + other[q, j, t]
        for o in FAR:
            spread(q, j, t, turn_z(o), z).start()

    def sum_e(q, j, t):
        spread(q, j, t, others, others).wait_recv()
        to_mate(q, j, t).start()

    def sum_f(q, j, t):
        to_mate(q, j, t).wait_recv()

        def step(k, _):
            full[q, j, t, k, pl.ds(4 * core, PART)] = total[q, j, t, k]
            full[q, j, t, k, pl.ds(4 * (1 - core), PART)] = mate[q, j, t, k]
            return 0

        lax.fori_loop(0, NZ, step, 0, unroll=2)

    mine = jnp.broadcast_to(owner_ref[0], (4, 128)) == band

    def load_tiles(c, _):
        lanes = pl.ds(pl.multiple_of(c * 128, 128), 128)
        for t in range(NT):
            tile = orb_ref[4 * t : 4 * t + 4, :, lanes]
            for j in range(NL):
                source[0, j, t, c // 9, c % 9] = jnp.where(mine, tile[:, j, :], 0.0)
        return 0

    for fetch in fetches[:NT]:
        fetch.wait()
    lax.fori_loop(0, LANES // 128, load_tiles, 0, unroll=8)
    pl.semaphore_wait(barrier, len(devices))
    for j in range(NL):
        for t in range(NT):
            sum_a(0, j, t)
    for t in range(NT):
        sum_b(0, 0, t)
    sum_b(0, 1, 0)
    for fetch in fetches[NT:]:
        fetch.wait()

    def square(value):
        value = jnp.where(value <= NG // 2, value, value - NG)
        return value * value

    lane = lax.broadcasted_iota(jnp.int32, (8, CHUNK), 1)
    lane_y = (lane * 683) >> 16
    flat = square(me * NX + lane_y) + square(lane - NG * lane_y)
    row = lax.broadcasted_iota(jnp.int32, (8, CHUNK), 0)

    def coulomb_rows(k, _):
        rows = pl.ds(pl.multiple_of(8 * k, 8), 8)
        squared = square(8 * k + row) + flat
        weight = mask_ref[rows, :].astype(F32)
        scale = -EXCHANGE_MIX * COULOMB / float(NG**3)
        coulomb[rows, :] = scale * weight / jnp.maximum(squared, 1).astype(F32)
        return 0

    lax.fori_loop(0, NG // 8, coulomb_rows, 0)

    def open_orb(a, _):
        for t in range(NT):
            tiles = []
            for k in range(3):
                lanes = pl.ds(pl.multiple_of(a * 384 + 128 * k, 128), 128)
                tiles.append(orb_ref[4 * t : 4 * t + 4, :, lanes].reshape(8, 128))
            quad = open_quad(*tiles)
            for b in range(4):
                orb_u[t, plane(4 * a + b), :] = quad[b]
        return 0

    lax.fori_loop(0, QUADS, open_orb, 0, unroll=2)

    def half_plane(y, j):
        return pl.ds(y * 8 + 4 * j, 4)

    def open_blk(j, t):
        def step(a, _):
            quad = open_quad(*[full[0, j, t, a // 3, (a % 3) * 3 + k] for k in range(3)])
            for b in range(4):
                blk_u[t, half_plane(4 * a + b, j), :] = quad[b]
            return 0

        lax.fori_loop(0, QUADS, step, 0, unroll=8)

    def transform_y(p0, p1):
        vh, vl = split(jnp.concatenate([p0, p1], axis=1))
        out = dot(weights[:192, :192], jnp.concatenate([vh, vl], axis=0))
        out = out[:NG] + out[NG:]
        return out[:, :128], out[:, 128:]

    def transform_z(value):
        vh, vl = split(value)
        out = dot(jnp.concatenate([vh, vl], axis=1), weights[192:448, :])
        return out[:, :128] + out[:, 128:]

    def forward(j, t):
        def rows(s, _):
            blk = blk_u[t, across(4 * j + s), :]
            out0, out1 = transform_y(
                orb_u[t, across(2 * s), :] * blk, orb_u[t, across(2 * s + 1), :] * blk
            )
            turned[across(2 * s), :] = out0
            turned[across(2 * s + 1), :] = out1
            return 0

        lax.fori_loop(0, 4, rows, 0, unroll=4)

        def half(h, _):
            out = transform_z(turned[pl.ds(pl.multiple_of(384 * h, 8), 384), :])
            for g in range(4):
                for s in range(3):
                    base = 96 * g + 32 * s
                    tiles = close_quad(*[out[base + 8 * b : base + 8 * b + 8] for b in range(4)])
                    for k in range(3):
                        lane = 384 * s + 128 * k
                        send_a[j, t, 4 * h + g, :, lane : lane + 128] = tiles[k]
            return 0

        lax.fori_loop(0, 2, half, 0)
        for o in range(1, NF):
            copy_a(j, t, turn(o), me).start()
        recv_a[j, t, me] = send_a[j, t, me]

    def middle(j):
        for t in range(NT):
            copy_a(j, t, others, others).wait_recv()

        def step(s, _):
            cols = pl.ds(pl.multiple_of(384 * s, 128), 384)
            value = recv_a[j, :, :, :, cols].reshape(NL * NG, 384)
            spectrum = left_product(weights[448:832, :192], value)
            weight = coulomb[:, cols]
            scaled = jnp.concatenate([spectrum[:NG] * weight, spectrum[NG:] * weight], axis=0)
            back = left_product(weights[832:1216, :192], scaled)
            send_b[j, :, :, :, cols] = back.reshape(NT, NF, 8, 384)
            return 0

        lax.fori_loop(0, 3, step, 0)
        for t in range(NT):
            for o in range(1, NF):
                copy_b(j, t, turn(o), me).start()
            recv_b[j, t, me] = send_b[j, t, me]

    def backward(j, t):
        copy_b(j, t, others, others).wait_recv()

        def half(h, _):
            planes = []
            for g in range(4):
                for s in range(3):
                    planes += open_quad(
                        *[
                            recv_b[j, t, 4 * h + g, :, 384 * s + 128 * k : 384 * s + 128 * k + 128]
                            for k in range(3)
                        ]
                    )
            out = transform_z(jnp.concatenate(planes, axis=0))
            turned[pl.ds(pl.multiple_of(384 * h, 8), 384), :] = out
            return 0

        lax.fori_loop(0, 2, half, 0)

        def rows(s, _):
            even, odd = across(2 * s), across(2 * s + 1)
            pot0, pot1 = transform_y(turned[even, :], turned[odd, :])
            blk = blk_u[t, across(4 * j + s), :]
            term0, term1 = blk * pot0, blk * pot1
            if j > 0:
                term0 = local_u[t, even, :] + term0
                term1 = local_u[t, odd, :] + term1
            local_u[t, even, :] = term0
            local_u[t, odd, :] = term1
            block_u[t, across(4 * j + s), :] = (
                orb_u[t, even, :] * pot0 + orb_u[t, odd, :] * pot1
            )
            return 0

        lax.fori_loop(0, 4, rows, 0, unroll=4)

    def close_block(j, t):
        def step(a, _):
            tiles = close_quad(*[block_u[t, half_plane(4 * a + b, j), :] for b in range(4)])
            for k in range(3):
                source[1, j, t, a // 3, (a % 3) * 3 + k] = tiles[k]
            return 0

        lax.fori_loop(0, QUADS, step, 0, unroll=8)

    def write_local(a, _):
        for t in range(NT):
            tiles = close_quad(*[local_u[t, plane(4 * a + b), :] for b in range(4)])
            for k in range(3):
                lanes = pl.ds(pl.multiple_of(a * 384 + 128 * k, 128), 128)
                local_ref[4 * t : 4 * t + 4, :, lanes] = tiles[k].reshape(4, NL, 128)
        return 0

    def write_half(j, t, piece, first):
        def step(k, _):
            for n in range(PART):
                lanes = pl.ds(pl.multiple_of((9 * k + first + n) * 128, 128), 128)
                block_ref[4 * t : 4 * t + 4, j, lanes] = piece[1, j, t, k, n]
            return 0

        lax.fori_loop(0, NZ, step, 0, unroll=2)

    def receive(j, t):
        sum_f(0, j, t)
        open_blk(j, t)
        forward(j, t)

    def finish(j, t):
        write_half(j, t, total, 4 * core)
        to_mate(1, j, t).wait_recv()
        write_half(j, t, mate, 4 * (1 - core))

    def block_out(t):
        return pltpu.make_async_copy(
            block_ref.at[pl.ds(4 * t, 4)], block_hbm.at[pl.ds(4 * t, 4)], out_sem.at[t]
        )

    sum_c(0, 0, 0)
    sum_c(0, 0, 1)
    sum_c(0, 0, 2)
    sum_d(0, 0, 0)
    sum_b(0, 1, 1)
    sum_c(0, 1, 0)
    sum_d(0, 0, 1)
    sum_b(0, 1, 2)
    sum_d(0, 0, 2)
    sum_e(0, 0, 0)
    sum_d(0, 1, 0)
    receive(0, 0)
    sum_c(0, 1, 1)
    sum_e(0, 0, 1)
    sum_c(0, 1, 2)
    receive(0, 1)
    sum_d(0, 1, 1)
    sum_e(0, 0, 2)
    sum_d(0, 1, 2)
    receive(0, 2)
    sum_e(0, 1, 0)
    receive(1, 0)
    sum_e(0, 1, 1)
    receive(1, 1)
    sum_e(0, 1, 2)
    receive(1, 2)

    def sum_sent(q, j, t):
        to_pair(q, j, t).wait_send()
        to_y(q, j, t).wait_send()
        to_mate(q, j, t).wait_send()
        scatter(q, j, t, others, others).wait_send()
        spread(q, j, t, others, others).wait_send()

    middle(0)
    for j in range(NL):
        for t in range(NT):
            sum_sent(0, j, t)
    middle(1)

    def back(j, t):
        backward(j, t)
        close_block(j, t)
        sum_a(1, j, t)

    back(0, 0)
    back(0, 1)
    sum_b(1, 0, 0)
    back(0, 2)
    sum_b(1, 0, 1)
    back(1, 0)
    sum_b(1, 0, 2)
    sum_c(1, 0, 0)
    back(1, 1)
    sum_b(1, 1, 0)
    sum_c(1, 0, 1)
    back(1, 2)
    sum_b(1, 1, 1)
    sum_c(1, 0, 2)
    sum_d(1, 0, 0)
    lax.fori_loop(0, QUADS // 2, write_local, 0, unroll=2)
    sum_b(1, 1, 2)
    lax.fori_loop(QUADS // 2, QUADS, write_local, 0, unroll=2)
    local_out = pltpu.make_async_copy(local_ref, local_hbm, out_sem.at[NT])
    local_out.start()
    sum_d(1, 0, 1)
    sum_c(1, 1, 0)
    sum_d(1, 0, 2)
    sum_c(1, 1, 1)
    sum_d(1, 1, 0)
    sum_c(1, 1, 2)
    sum_d(1, 1, 1)
    sum_d(1, 1, 2)
    for t in range(NT):
        sum_e(1, 0, t)
    for t in range(NT):
        finish(0, t)
    for j in range(NL):
        for t in range(NT):
            copy_a(j, t, others, others).wait_send()
            copy_b(j, t, others, others).wait_send()
    for t in range(NT):
        sum_e(1, 1, t)
        if t > 0:
            finish(1, t - 1)
            block_out(t - 1).start()
    finish(1, NT - 1)
    block_out(NT - 1).start()
    for j in range(NL):
        for t in range(NT):
            sum_sent(1, j, t)
    local_out.wait()
    for t in range(NT):
        block_out(t).wait()


def per_device(orbitals, owners, cutoff_mask):
    dma = pltpu.SemaphoreType.DMA

    def buffer(*shape):
        return pltpu.VMEM(shape, F32)

    def like(array):
        return pltpu.VMEM(array.shape, array.dtype)

    planes = buffer(NT, PLANES, 128)
    tiles = buffer(2, NL, NT, NZ, 9, 4, 128)
    pieces = buffer(2, NL, NT, NZ, PART, 4, 128)
    single = buffer(2, NL, NT, PART, 4, 128)
    grid = buffer(NL, NT, NF, 8, CHUNK)
    constants = jnp.asarray(tables())
    flat = jax.ShapeDtypeStruct((NX, NL, LANES), F32)
    many = dma((NL, NT))
    few = dma((2, NL, NT))
    anywhere = pl.BlockSpec(memory_space=pl.ANY)
    stay = pl.BlockSpec(memory_space=pltpu.HBM)
    orb = orbitals.transpose(1, 0, 2)
    local, block = pl.pallas_call(
        kernel,
        out_shape=(flat, flat),
        in_specs=[stay, pl.BlockSpec(memory_space=pltpu.SMEM)]
        + [stay] * 2,
        out_specs=(anywhere, anywhere),
        scratch_shapes=[
            like(orb), like(cutoff_mask), like(constants),
            like(flat), like(flat), dma((NT + 2,)), dma((NT + 1,)),
            buffer(NG, CHUNK), tiles, tiles, planes, planes,
            buffer(PLANES, 128), planes, planes, grid, grid, grid, grid,
            pieces, pieces, pieces, single, single, pieces, pieces,
            many, many, many, many, few, few, few, few, few, few, few, few, few, few,
        ],
        compiler_params=pltpu.CompilerParams(
            collective_id=0, has_side_effects=True, vmem_limit_bytes=60 << 20
        ),
    )(orb, owners, cutoff_mask, constants)
    return local.transpose(1, 0, 2), block.transpose(1, 0, 2)


def solution(mesh):
    in_specs = (P("band", "fft", None), P(), P(None, "fft"))
    out_specs = (P("band", "fft", None), P(None, "fft", None))
    return jax.shard_map(
        per_device, mesh=mesh, in_specs=in_specs, out_specs=out_specs, check_vma=False
    )
```

```python
import math

import jax
import jax.numpy as jnp
import numpy as np
from jax import lax
from jax.experimental import pallas as pl
from jax.experimental.pallas import tpu as pltpu
from jax.sharding import PartitionSpec as P

COULOMB = 400.0
EXCHANGE_MIX = 0.25
NG = 96
NL = 2
NX = 12
NF = 8
NZ = 8
NT = 3
LANES = NG * NG
CHUNK = NX * NG
QUADS = NG // 4
PLANES = NG * 8
PART = 5
MESH = pl.DeviceIdType.MESH
F32 = jnp.float32
BF16 = jnp.bfloat16
FAR = (4, 3, 5, 2, 6, 1, 7)


def split_const(matrix):
    high = matrix.astype(np.float32).astype(jnp.bfloat16)
    low = (matrix.astype(np.float64) - np.asarray(high, np.float64)).astype(jnp.bfloat16)
    return np.asarray(high), np.asarray(low)


def tables():
    index = np.arange(NG)
    angle = 2.0 * math.pi * (index[:, None] * index[None, :] % NG) / NG
    cas = np.cos(angle) + np.sin(angle)
    cas_h, cas_l = split_const(cas)
    zero = np.zeros_like(cas_h)
    left_y = np.concatenate(
        [np.concatenate([cas_h, cas_h], 1), np.concatenate([cas_l, zero], 1)], 0
    )
    right_z = np.zeros((256, 256), cas_h.dtype)
    right_z[:NG, :NG] = cas_h
    right_z[128 : 128 + NG, :NG] = cas_h
    right_z[:NG, 128 : 128 + NG] = cas_l
    both = np.zeros((NL, NG, NT, NF, 4, NL))
    for i in range(NL):
        both[i, :, :, :, :, i] = cas.reshape(NG, NF, NT, 4).transpose(0, 2, 1, 3)
    both = both.reshape(NL * NG, NL * NG)
    left_fx = np.concatenate(split_const(both), 0)
    left_bx = np.concatenate(split_const(both.T), 0)
    packed = np.zeros((1216, 256), cas_h.dtype)
    packed[:192, :192] = left_y
    packed[192:448] = right_z
    packed[448:832, :192] = left_fx
    packed[832:1216, :192] = left_bx
    return packed


def dot(a, b):
    return lax.dot_general(a, b, (((1,), (0,)), ((), ())), preferred_element_type=F32)


def split(value):
    high = value.astype(BF16)
    low = (value - high.astype(F32)).astype(BF16)
    return high, low


def left_product(left, value):
    rows = left.shape[0] // 2
    vh, vl = split(value)
    first = dot(left, vh)
    return first[:rows] + first[rows:] + dot(left[:rows], vl)


def open_quad(c0, c1, c2):
    lane = lax.broadcasted_iota(jnp.int32, c0.shape, 1)
    y1 = jnp.where(lane < 32, pltpu.roll(c0, 32, 1), pltpu.roll(c1, 32, 1))
    y2 = jnp.where(lane < 64, pltpu.roll(c1, 64, 1), pltpu.roll(c2, 64, 1))
    return c0, y1, y2, pltpu.roll(c2, 96, 1)


def close_quad(e0, e1, e2, e3):
    lane = lax.broadcasted_iota(jnp.int32, e0.shape, 1)
    r1 = pltpu.roll(e1, 96, 1)
    r2 = pltpu.roll(e2, 64, 1)
    r3 = pltpu.roll(e3, 32, 1)
    c0 = jnp.where(lane < 96, e0, r1)
    c1 = jnp.where(lane < 64, r1, r2)
    c2 = jnp.where(lane < 32, r2, r3)
    return c0, c1, c2


def plane(y):
    return pl.ds(pl.multiple_of(y * 8, 8), 8)


def across(row):
    return pl.ds(row, NG, stride=8)


def kernel(
    orb_hbm, owner_ref, mask_hbm, weights_hbm, local_hbm, block_hbm,
    orb_ref, mask_ref, weights,
    local_ref, block_ref, in_sem, out_sem,
    coulomb, source, full, orb_u, blk_u, turned, local_u, block_u,
    send_a, recv_a, send_b, recv_b, pair, part, gathered, summed, other, total, mate,
    sa_sem, ra_sem, sb_sem, rb_sem, ps_sem, pr_sem, ys_sem, yr_sem,
    zs_sem, zr_sem, gs_sem, gr_sem, ms_sem, mr_sem,
):
    me = lax.axis_index("fft")
    band = lax.axis_index("band")
    core = lax.rem(band, 2)
    z = lax.rem(band // 2, NZ)
    yh = band // (2 * NZ)
    mate_band = band + 1 - 2 * core
    y_band = lax.rem(band + 2 * NZ, 4 * NZ)

    def z_band(other_z):
        return (yh * NZ + other_z) * 2 + core

    def turn(o):
        return lax.rem(me + o, NF)

    def turn_z(o):
        return lax.rem(z + o, NZ)

    fetches = []
    for t in range(NT):
        rows = pl.ds(4 * t, 4)
        fetches.append(
            pltpu.make_async_copy(orb_hbm.at[rows], orb_ref.at[rows], in_sem.at[t])
        )
    fetches.append(pltpu.make_async_copy(mask_hbm, mask_ref, in_sem.at[NT]))
    fetches.append(pltpu.make_async_copy(weights_hbm, weights, in_sem.at[NT + 1]))
    for fetch in fetches:
        fetch.start()
    barrier = pltpu.get_barrier_semaphore()
    devices = [{"fft": turn(o)} for o in range(1, NF)]
    devices += [{"band": mate_band}, {"band": y_band}]
    devices += [{"band": z_band(turn_z(o))} for o in range(1, NZ)]
    for device in devices:
        pl.semaphore_signal(barrier, inc=1, device_id=device, device_id_type=MESH)

    def remote(src, dst, send, recv, device):
        return pltpu.make_async_remote_copy(
            src_ref=src, dst_ref=dst, send_sem=send, recv_sem=recv,
            device_id=device, device_id_type=MESH,
        )

    others = pl.ds(0, NF - 1)

    def copy_a(j, t, peer, slot):
        return remote(
            send_a.at[j, t, peer], recv_a.at[j, t, slot],
            sa_sem.at[j, t], ra_sem.at[j, t], {"fft": turn(1) if peer is others else peer},
        )

    def copy_b(j, t, peer, slot):
        return remote(
            send_b.at[j, t, peer], recv_b.at[j, t, slot],
            sb_sem.at[j, t], rb_sem.at[j, t], {"fft": turn(1) if peer is others else peer},
        )

    def to_pair(q, j, t):
        return remote(
            source.at[q, j, t, :, pl.ds(4 * (1 - core), PART)], pair.at[q, j, t],
            ps_sem.at[q, j, t], pr_sem.at[q, j, t], {"band": mate_band},
        )

    def scatter(q, j, t, peer, slot):
        return remote(
            part.at[q, j, t, peer], gathered.at[q, j, t, slot],
            zs_sem.at[q, j, t], zr_sem.at[q, j, t],
            {"band": z_band(turn_z(1) if peer is others else peer)},
        )

    def to_y(q, j, t):
        return remote(
            summed.at[q, j, t], other.at[q, j, t],
            ys_sem.at[q, j, t], yr_sem.at[q, j, t], {"band": y_band},
        )

    def spread(q, j, t, peer, slot):
        return remote(
            total.at[q, j, t, slot], total.at[q, j, t, slot],
            gs_sem.at[q, j, t], gr_sem.at[q, j, t],
            {"band": z_band(turn_z(1) if peer is others else peer)},
        )

    def to_mate(q, j, t):
        return remote(
            total.at[q, j, t], mate.at[q, j, t],
            ms_sem.at[q, j, t], mr_sem.at[q, j, t], {"band": mate_band},
        )

    def sum_a(q, j, t):
        to_pair(q, j, t).start()

    def sum_b(q, j, t):
        to_pair(q, j, t).wait_recv()

        def step(k, _):
            part[q, j, t, k] = source[q, j, t, k, pl.ds(4 * core, PART)] + pair[q, j, t, k]
            return 0

        lax.fori_loop(0, NZ, step, 0, unroll=2)
        for o in FAR:
            scatter(q, j, t, turn_z(o), z).start()
        gathered[q, j, t, z] = part[q, j, t, z]

    def sum_c(q, j, t):
        scatter(q, j, t, others, others).wait_recv()
        value = gathered[q, j, t, 0]
        for k in range(1, NZ):
            value = value + gathered[q, j, t, k]
        summed[q, j, t] = value
        to_y(q, j, t).start()

    def sum_d(q, j, t):
        to_y(q, j, t).wait_recv()
        total[q, j, t, z] = summed[q, j, t] + other[q, j, t]
        for o in FAR:
            spread(q, j, t, turn_z(o), z).start()

    def sum_e(q, j, t):
        spread(q, j, t, others, others).wait_recv()
        to_mate(q, j, t).start()

    def sum_f(q, j, t):
        to_mate(q, j, t).wait_recv()

        def step(k, _):
            full[q, j, t, k, pl.ds(4 * core, PART)] = total[q, j, t, k]
            full[q, j, t, k, pl.ds(4 * (1 - core), PART)] = mate[q, j, t, k]
            return 0

        lax.fori_loop(0, NZ, step, 0, unroll=2)

    mine = jnp.broadcast_to(owner_ref[0], (4, 128)) == band

    def load_tiles(c, _):
        lanes = pl.ds(pl.multiple_of(c * 128, 128), 128)
        for t in range(NT):
            tile = orb_ref[4 * t : 4 * t + 4, :, lanes]
            for j in range(NL):
                source[0, j, t, c // 9, c % 9] = jnp.where(mine, tile[:, j, :], 0.0)
        return 0

    for fetch in fetches[:NT]:
        fetch.wait()
    lax.fori_loop(0, LANES // 128, load_tiles, 0, unroll=8)
    pl.semaphore_wait(barrier, len(devices))
    for j in range(NL):
        for t in range(NT):
            sum_a(0, j, t)
    for t in range(NT):
        sum_b(0, 0, t)
    sum_b(0, 1, 0)
    for fetch in fetches[NT:]:
        fetch.wait()

    def square(value):
        value = jnp.where(value <= NG // 2, value, value - NG)
        return value * value

    lane = lax.broadcasted_iota(jnp.int32, (8, CHUNK), 1)
    lane_y = (lane * 683) >> 16
    flat = square(me * NX + lane_y) + square(lane - NG * lane_y)
    row = lax.broadcasted_iota(jnp.int32, (8, CHUNK), 0)

    def coulomb_rows(k, _):
        rows = pl.ds(pl.multiple_of(8 * k, 8), 8)
        squared = square(8 * k + row) + flat
        weight = mask_ref[rows, :].astype(F32)
        scale = -EXCHANGE_MIX * COULOMB / float(NG**3)
        coulomb[rows, :] = scale * weight / jnp.maximum(squared, 1).astype(F32)
        return 0

    lax.fori_loop(0, NG // 8, coulomb_rows, 0)

    def open_orb(a, _):
        for t in range(NT):
            tiles = []
            for k in range(3):
                lanes = pl.ds(pl.multiple_of(a * 384 + 128 * k, 128), 128)
                tiles.append(orb_ref[4 * t : 4 * t + 4, :, lanes].reshape(8, 128))
            quad = open_quad(*tiles)
            for b in range(4):
                orb_u[t, plane(4 * a + b), :] = quad[b]
        return 0

    lax.fori_loop(0, QUADS, open_orb, 0, unroll=2)

    def half_plane(y, j):
        return pl.ds(y * 8 + 4 * j, 4)

    def open_blk(j, t):
        def step(a, _):
            quad = open_quad(*[full[0, j, t, a // 3, (a % 3) * 3 + k] for k in range(3)])
            for b in range(4):
                blk_u[t, half_plane(4 * a + b, j), :] = quad[b]
            return 0

        lax.fori_loop(0, QUADS, step, 0, unroll=8)

    def transform_y(p0, p1):
        vh, vl = split(jnp.concatenate([p0, p1], axis=1))
        out = dot(weights[:192, :192], jnp.concatenate([vh, vl], axis=0))
        out = out[:NG] + out[NG:]
        return out[:, :128], out[:, 128:]

    def transform_z(value):
        vh, vl = split(value)
        out = dot(jnp.concatenate([vh, vl], axis=1), weights[192:448, :])
        return out[:, :128] + out[:, 128:]

    def forward(j, t):
        def rows(s, _):
            blk = blk_u[t, across(4 * j + s), :]
            out0, out1 = transform_y(
                orb_u[t, across(2 * s), :] * blk, orb_u[t, across(2 * s + 1), :] * blk
            )
            turned[across(2 * s), :] = out0
            turned[across(2 * s + 1), :] = out1
            return 0

        lax.fori_loop(0, 4, rows, 0, unroll=4)

        def half(h, _):
            out = transform_z(turned[pl.ds(pl.multiple_of(384 * h, 8), 384), :])
            for g in range(4):
                for s in range(3):
                    base = 96 * g + 32 * s
                    tiles = close_quad(*[out[base + 8 * b : base + 8 * b + 8] for b in range(4)])
                    for k in range(3):
                        lane = 384 * s + 128 * k
                        send_a[j, t, 4 * h + g, :, lane : lane + 128] = tiles[k]
            return 0

        lax.fori_loop(0, 2, half, 0)
        for o in range(1, NF):
            copy_a(j, t, turn(o), me).start()
        recv_a[j, t, me] = send_a[j, t, me]

    def middle(j):
        for t in range(NT):
            copy_a(j, t, others, others).wait_recv()

        def step(s, _):
            cols = pl.ds(pl.multiple_of(384 * s, 128), 384)
            value = recv_a[j, :, :, :, cols].reshape(NL * NG, 384)
            spectrum = left_product(weights[448:832, :192], value)
            weight = coulomb[:, cols]
            scaled = jnp.concatenate([spectrum[:NG] * weight, spectrum[NG:] * weight], axis=0)
            back = left_product(weights[832:1216, :192], scaled)
            send_b[j, :, :, :, cols] = back.reshape(NT, NF, 8, 384)
            return 0

        lax.fori_loop(0, 3, step, 0)
        for t in range(NT):
            for o in range(1, NF):
                copy_b(j, t, turn(o), me).start()
            recv_b[j, t, me] = send_b[j, t, me]

    def backward(j, t):
        copy_b(j, t, others, others).wait_recv()

        def half(h, _):
            planes = []
            for g in range(4):
                for s in range(3):
                    planes += open_quad(
                        *[
                            recv_b[j, t, 4 * h + g, :, 384 * s + 128 * k : 384 * s + 128 * k + 128]
                            for k in range(3)
                        ]
                    )
            out = transform_z(jnp.concatenate(planes, axis=0))
            turned[pl.ds(pl.multiple_of(384 * h, 8), 384), :] = out
            return 0

        lax.fori_loop(0, 2, half, 0)

        def rows(s, _):
            even, odd = across(2 * s), across(2 * s + 1)
            pot0, pot1 = transform_y(turned[even, :], turned[odd, :])
            blk = blk_u[t, across(4 * j + s), :]
            term0, term1 = blk * pot0, blk * pot1
            if j > 0:
                term0 = local_u[t, even, :] + term0
                term1 = local_u[t, odd, :] + term1
            local_u[t, even, :] = term0
            local_u[t, odd, :] = term1
            block_u[t, across(4 * j + s), :] = (
                orb_u[t, even, :] * pot0 + orb_u[t, odd, :] * pot1
            )
            return 0

        lax.fori_loop(0, 4, rows, 0, unroll=4)

    def close_block(j, t):
        def step(a, _):
            tiles = close_quad(*[block_u[t, half_plane(4 * a + b, j), :] for b in range(4)])
            for k in range(3):
                source[1, j, t, a // 3, (a % 3) * 3 + k] = tiles[k]
            return 0

        lax.fori_loop(0, QUADS, step, 0, unroll=8)

    def write_local(a, _):
        for t in range(NT):
            tiles = close_quad(*[local_u[t, plane(4 * a + b), :] for b in range(4)])
            for k in range(3):
                lanes = pl.ds(pl.multiple_of(a * 384 + 128 * k, 128), 128)
                local_ref[4 * t : 4 * t + 4, :, lanes] = tiles[k].reshape(4, NL, 128)
        return 0

    def write_half(j, t, piece, first):
        def step(k, _):
            for n in range(PART):
                lanes = pl.ds(pl.multiple_of((9 * k + first + n) * 128, 128), 128)
                block_ref[4 * t : 4 * t + 4, j, lanes] = piece[1, j, t, k, n]
            return 0

        lax.fori_loop(0, NZ, step, 0, unroll=2)

    def receive(j, t):
        sum_f(0, j, t)
        open_blk(j, t)
        forward(j, t)

    def finish(j, t):
        write_half(j, t, total, 4 * core)
        to_mate(1, j, t).wait_recv()
        write_half(j, t, mate, 4 * (1 - core))

    def block_out(t):
        return pltpu.make_async_copy(
            block_ref.at[pl.ds(4 * t, 4)], block_hbm.at[pl.ds(4 * t, 4)], out_sem.at[t]
        )

    sum_c(0, 0, 0)
    sum_c(0, 0, 1)
    sum_c(0, 0, 2)
    sum_d(0, 0, 0)
    sum_b(0, 1, 1)
    sum_c(0, 1, 0)
    sum_d(0, 0, 1)
    sum_b(0, 1, 2)
    sum_d(0, 0, 2)
    sum_e(0, 0, 0)
    sum_d(0, 1, 0)
    receive(0, 0)
    sum_c(0, 1, 1)
    sum_e(0, 0, 1)
    sum_c(0, 1, 2)
    receive(0, 1)
    sum_d(0, 1, 1)
    sum_e(0, 0, 2)
    sum_d(0, 1, 2)
    receive(0, 2)
    sum_e(0, 1, 0)
    receive(1, 0)
    sum_e(0, 1, 1)
    receive(1, 1)
    sum_e(0, 1, 2)
    receive(1, 2)

    def sum_sent(q, j, t):
        to_pair(q, j, t).wait_send()
        to_y(q, j, t).wait_send()
        to_mate(q, j, t).wait_send()
        scatter(q, j, t, others, others).wait_send()
        spread(q, j, t, others, others).wait_send()

    middle(0)
    for j in range(NL):
        for t in range(NT):
            sum_sent(0, j, t)
    middle(1)

    def back(j, t):
        backward(j, t)
        close_block(j, t)
        sum_a(1, j, t)

    back(0, 0)
    sum_b(1, 0, 0)
    back(0, 1)
    sum_b(1, 0, 1)
    back(0, 2)
    sum_b(1, 0, 2)
    sum_c(1, 0, 0)
    back(1, 0)
    sum_b(1, 1, 0)
    sum_c(1, 0, 1)
    back(1, 1)
    sum_b(1, 1, 1)
    sum_c(1, 0, 2)
    sum_d(1, 0, 0)
    back(1, 2)
    lax.fori_loop(0, QUADS // 2, write_local, 0, unroll=2)
    sum_b(1, 1, 2)
    sum_d(1, 0, 1)
    sum_c(1, 1, 0)
    sum_d(1, 0, 2)
    lax.fori_loop(QUADS // 2, QUADS, write_local, 0, unroll=2)
    local_out = pltpu.make_async_copy(local_ref, local_hbm, out_sem.at[NT])
    local_out.start()
    sum_c(1, 1, 1)
    sum_d(1, 1, 0)
    sum_c(1, 1, 2)
    sum_d(1, 1, 1)
    sum_d(1, 1, 2)
    for t in range(NT):
        sum_e(1, 0, t)
    for t in range(NT):
        finish(0, t)
    for j in range(NL):
        for t in range(NT):
            copy_a(j, t, others, others).wait_send()
            copy_b(j, t, others, others).wait_send()
    for t in range(NT):
        sum_e(1, 1, t)
        if t > 0:
            finish(1, t - 1)
            block_out(t - 1).start()
    finish(1, NT - 1)
    block_out(NT - 1).start()
    for j in range(NL):
        for t in range(NT):
            sum_sent(1, j, t)
    local_out.wait()
    for t in range(NT):
        block_out(t).wait()


def per_device(orbitals, owners, cutoff_mask):
    dma = pltpu.SemaphoreType.DMA

    def buffer(*shape):
        return pltpu.VMEM(shape, F32)

    def like(array):
        return pltpu.VMEM(array.shape, array.dtype)

    planes = buffer(NT, PLANES, 128)
    tiles = buffer(2, NL, NT, NZ, 9, 4, 128)
    pieces = buffer(2, NL, NT, NZ, PART, 4, 128)
    single = buffer(2, NL, NT, PART, 4, 128)
    grid = buffer(NL, NT, NF, 8, CHUNK)
    constants = jnp.asarray(tables())
    flat = jax.ShapeDtypeStruct((NX, NL, LANES), F32)
    many = dma((NL, NT))
    few = dma((2, NL, NT))
    anywhere = pl.BlockSpec(memory_space=pl.ANY)
    stay = pl.BlockSpec(memory_space=pltpu.HBM)
    orb = orbitals.transpose(1, 0, 2)
    local, block = pl.pallas_call(
        kernel,
        out_shape=(flat, flat),
        in_specs=[stay, pl.BlockSpec(memory_space=pltpu.SMEM)]
        + [stay] * 2,
        out_specs=(anywhere, anywhere),
        scratch_shapes=[
            like(orb), like(cutoff_mask), like(constants),
            like(flat), like(flat), dma((NT + 2,)), dma((NT + 1,)),
            buffer(NG, CHUNK), tiles, tiles, planes, planes,
            buffer(PLANES, 128), planes, planes, grid, grid, grid, grid,
            pieces, pieces, pieces, single, single, pieces, pieces,
            many, many, many, many, few, few, few, few, few, few, few, few, few, few,
        ],
        compiler_params=pltpu.CompilerParams(
            collective_id=0, has_side_effects=True, vmem_limit_bytes=60 << 20
        ),
    )(orb, owners, cutoff_mask, constants)
    return local.transpose(1, 0, 2), block.transpose(1, 0, 2)


def solution(mesh):
    in_specs = (P("band", "fft", None), P(), P(None, "fft"))
    out_specs = (P("band", "fft", None), P(None, "fft", None))
    return jax.shard_map(
        per_device, mesh=mesh, in_specs=in_specs, out_specs=out_specs, check_vma=False
    )
```

```python
import math

import jax
import jax.numpy as jnp
import numpy as np
from jax import lax
from jax.experimental import pallas as pl
from jax.experimental.pallas import tpu as pltpu
from jax.sharding import PartitionSpec as P

COULOMB = 400.0
EXCHANGE_MIX = 0.25
NG = 96
NL = 2
NX = 12
NF = 8
NZ = 8
NT = 3
LANES = NG * NG
CHUNK = NX * NG
QUADS = NG // 4
PLANES = NG * 8
PART = 5
MESH = pl.DeviceIdType.MESH
F32 = jnp.float32
BF16 = jnp.bfloat16
FAR = (4, 3, 5, 2, 6, 1, 7)


def split_const(matrix):
    high = matrix.astype(np.float32).astype(jnp.bfloat16)
    low = (matrix.astype(np.float64) - np.asarray(high, np.float64)).astype(jnp.bfloat16)
    return np.asarray(high), np.asarray(low)


def tables():
    index = np.arange(NG)
    angle = 2.0 * math.pi * (index[:, None] * index[None, :] % NG) / NG
    cas = np.cos(angle) + np.sin(angle)
    cas_h, cas_l = split_const(cas)
    zero = np.zeros_like(cas_h)
    left_y = np.concatenate(
        [np.concatenate([cas_h, cas_h], 1), np.concatenate([cas_l, zero], 1)], 0
    )
    right_z = np.zeros((256, 256), cas_h.dtype)
    right_z[:NG, :NG] = cas_h
    right_z[128 : 128 + NG, :NG] = cas_h
    right_z[:NG, 128 : 128 + NG] = cas_l
    both = np.zeros((NL, NG, NT, NF, 4, NL))
    for i in range(NL):
        both[i, :, :, :, :, i] = cas.reshape(NG, NF, NT, 4).transpose(0, 2, 1, 3)
    both = both.reshape(NL * NG, NL * NG)
    left_fx = np.concatenate(split_const(both), 0)
    left_bx = np.concatenate(split_const(both.T), 0)
    packed = np.zeros((1216, 256), cas_h.dtype)
    packed[:192, :192] = left_y
    packed[192:448] = right_z
    packed[448:832, :192] = left_fx
    packed[832:1216, :192] = left_bx
    return packed


def dot(a, b):
    return lax.dot_general(a, b, (((1,), (0,)), ((), ())), preferred_element_type=F32)


def split(value):
    high = value.astype(BF16)
    low = (value - high.astype(F32)).astype(BF16)
    return high, low


def left_product(left, value):
    rows = left.shape[0] // 2
    vh, vl = split(value)
    first = dot(left, vh)
    return first[:rows] + first[rows:] + dot(left[:rows], vl)


def open_quad(c0, c1, c2):
    lane = lax.broadcasted_iota(jnp.int32, c0.shape, 1)
    y1 = jnp.where(lane < 32, pltpu.roll(c0, 32, 1), pltpu.roll(c1, 32, 1))
    y2 = jnp.where(lane < 64, pltpu.roll(c1, 64, 1), pltpu.roll(c2, 64, 1))
    return c0, y1, y2, pltpu.roll(c2, 96, 1)


def close_quad(e0, e1, e2, e3):
    lane = lax.broadcasted_iota(jnp.int32, e0.shape, 1)
    r1 = pltpu.roll(e1, 96, 1)
    r2 = pltpu.roll(e2, 64, 1)
    r3 = pltpu.roll(e3, 32, 1)
    c0 = jnp.where(lane < 96, e0, r1)
    c1 = jnp.where(lane < 64, r1, r2)
    c2 = jnp.where(lane < 32, r2, r3)
    return c0, c1, c2


def plane(y):
    return pl.ds(pl.multiple_of(y * 8, 8), 8)


def across(row):
    return pl.ds(row, NG, stride=8)


def kernel(
    orb_hbm, owner_ref, mask_hbm, weights_hbm, local_hbm, block_hbm,
    orb_ref, mask_ref, weights,
    local_ref, block_ref, in_sem, out_sem,
    coulomb, source, full, orb_u, blk_u, turned, local_u, block_u,
    send_a, recv_a, send_b, recv_b, pair, part, gathered, summed, other, total, mate,
    sa_sem, ra_sem, sb_sem, rb_sem, ps_sem, pr_sem, ys_sem, yr_sem,
    zs_sem, zr_sem, gs_sem, gr_sem, ms_sem, mr_sem,
):
    me = lax.axis_index("fft")
    band = lax.axis_index("band")
    core = lax.rem(band, 2)
    z = lax.rem(band // 2, NZ)
    yh = band // (2 * NZ)
    mate_band = band + 1 - 2 * core
    y_band = lax.rem(band + 2 * NZ, 4 * NZ)

    def z_band(other_z):
        return (yh * NZ + other_z) * 2 + core

    def turn(o):
        return lax.rem(me + o, NF)

    def turn_z(o):
        return lax.rem(z + o, NZ)

    fetches = []
    for t in range(NT):
        rows = pl.ds(4 * t, 4)
        fetches.append(
            pltpu.make_async_copy(orb_hbm.at[rows], orb_ref.at[rows], in_sem.at[t])
        )
    fetches.append(pltpu.make_async_copy(mask_hbm, mask_ref, in_sem.at[NT]))
    fetches.append(pltpu.make_async_copy(weights_hbm, weights, in_sem.at[NT + 1]))
    for fetch in fetches:
        fetch.start()
    barrier = pltpu.get_barrier_semaphore()
    devices = [{"fft": turn(o)} for o in range(1, NF)]
    devices += [{"band": mate_band}, {"band": y_band}]
    devices += [{"band": z_band(turn_z(o))} for o in range(1, NZ)]
    for device in devices:
        pl.semaphore_signal(barrier, inc=1, device_id=device, device_id_type=MESH)

    def remote(src, dst, send, recv, device):
        return pltpu.make_async_remote_copy(
            src_ref=src, dst_ref=dst, send_sem=send, recv_sem=recv,
            device_id=device, device_id_type=MESH,
        )

    others = pl.ds(0, NF - 1)

    def copy_a(j, t, peer, slot):
        return remote(
            send_a.at[j, t, peer], recv_a.at[j, t, slot],
            sa_sem.at[j, t], ra_sem.at[j, t], {"fft": turn(1) if peer is others else peer},
        )

    def copy_b(j, t, peer, slot):
        return remote(
            send_b.at[j, t, peer], recv_b.at[j, t, slot],
            sb_sem.at[j, t], rb_sem.at[j, t], {"fft": turn(1) if peer is others else peer},
        )

    def to_pair(q, j, t):
        return remote(
            source.at[q, j, t, :, pl.ds(4 * (1 - core), PART)], pair.at[q, j, t],
            ps_sem.at[q, j, t], pr_sem.at[q, j, t], {"band": mate_band},
        )

    def scatter(q, j, t, peer, slot):
        return remote(
            part.at[q, j, t, peer], gathered.at[q, j, t, slot],
            zs_sem.at[q, j, t], zr_sem.at[q, j, t],
            {"band": z_band(turn_z(1) if peer is others else peer)},
        )

    def to_y(q, j, t):
        return remote(
            summed.at[q, j, t], other.at[q, j, t],
            ys_sem.at[q, j, t], yr_sem.at[q, j, t], {"band": y_band},
        )

    def spread(q, j, t, peer, slot):
        return remote(
            total.at[q, j, t, slot], total.at[q, j, t, slot],
            gs_sem.at[q, j, t], gr_sem.at[q, j, t],
            {"band": z_band(turn_z(1) if peer is others else peer)},
        )

    def to_mate(q, j, t):
        return remote(
            total.at[q, j, t], mate.at[q, j, t],
            ms_sem.at[q, j, t], mr_sem.at[q, j, t], {"band": mate_band},
        )

    def sum_a(q, j, t):
        to_pair(q, j, t).start()

    def sum_b(q, j, t):
        to_pair(q, j, t).wait_recv()

        def step(k, _):
            part[q, j, t, k] = source[q, j, t, k, pl.ds(4 * core, PART)] + pair[q, j, t, k]
            return 0

        lax.fori_loop(0, NZ, step, 0, unroll=2)
        for o in FAR:
            scatter(q, j, t, turn_z(o), z).start()
        gathered[q, j, t, z] = part[q, j, t, z]

    def sum_c(q, j, t):
        scatter(q, j, t, others, others).wait_recv()
        value = gathered[q, j, t, 0]
        for k in range(1, NZ):
            value = value + gathered[q, j, t, k]
        summed[q, j, t] = value
        to_y(q, j, t).start()

    def sum_d(q, j, t):
        to_y(q, j, t).wait_recv()
        total[q, j, t, z] = summed[q, j, t] + other[q, j, t]
        for o in FAR:
            spread(q, j, t, turn_z(o), z).start()

    def sum_e(q, j, t):
        spread(q, j, t, others, others).wait_recv()
        to_mate(q, j, t).start()

    def sum_f(q, j, t):
        to_mate(q, j, t).wait_recv()

        def step(k, _):
            full[q, j, t, k, pl.ds(4 * core, PART)] = total[q, j, t, k]
            full[q, j, t, k, pl.ds(4 * (1 - core), PART)] = mate[q, j, t, k]
            return 0

        lax.fori_loop(0, NZ, step, 0, unroll=2)

    mine = jnp.broadcast_to(owner_ref[0], (4, 128)) == band

    def load_tiles(c, _):
        lanes = pl.ds(pl.multiple_of(c * 128, 128), 128)
        for t in range(NT):
            tile = orb_ref[4 * t : 4 * t + 4, :, lanes]
            for j in range(NL):
                source[0, j, t, c // 9, c % 9] = jnp.where(mine, tile[:, j, :], 0.0)
        return 0

    for fetch in fetches[:NT]:
        fetch.wait()
    lax.fori_loop(0, LANES // 128, load_tiles, 0, unroll=8)
    pl.semaphore_wait(barrier, len(devices))
    for j in range(NL):
        for t in range(NT):
            sum_a(0, j, t)
    for t in range(NT):
        sum_b(0, 0, t)
    sum_b(0, 1, 0)
    for fetch in fetches[NT:]:
        fetch.wait()

    def square(value):
        value = jnp.where(value <= NG // 2, value, value - NG)
        return value * value

    lane = lax.broadcasted_iota(jnp.int32, (8, CHUNK), 1)
    lane_y = (lane * 683) >> 16
    flat = square(me * NX + lane_y) + square(lane - NG * lane_y)
    row = lax.broadcasted_iota(jnp.int32, (8, CHUNK), 0)

    def coulomb_rows(k, _):
        rows = pl.ds(pl.multiple_of(8 * k, 8), 8)
        squared = square(8 * k + row) + flat
        weight = mask_ref[rows, :].astype(F32)
        scale = -EXCHANGE_MIX * COULOMB / float(NG**3)
        coulomb[rows, :] = scale * weight / jnp.maximum(squared, 1).astype(F32)
        return 0

    lax.fori_loop(0, NG // 8, coulomb_rows, 0)

    def open_orb(a, _):
        for t in range(NT):
            tiles = []
            for k in range(3):
                lanes = pl.ds(pl.multiple_of(a * 384 + 128 * k, 128), 128)
                tiles.append(orb_ref[4 * t : 4 * t + 4, :, lanes].reshape(8, 128))
            quad = open_quad(*tiles)
            for b in range(4):
                orb_u[t, plane(4 * a + b), :] = quad[b]
        return 0

    lax.fori_loop(0, QUADS, open_orb, 0, unroll=2)

    def half_plane(y, j):
        return pl.ds(y * 8 + 4 * j, 4)

    def open_blk(j, t):
        def step(a, _):
            quad = open_quad(*[full[0, j, t, a // 3, (a % 3) * 3 + k] for k in range(3)])
            for b in range(4):
                blk_u[t, half_plane(4 * a + b, j), :] = quad[b]
            return 0

        lax.fori_loop(0, QUADS, step, 0, unroll=8)

    def transform_y(p0, p1):
        vh, vl = split(jnp.concatenate([p0, p1], axis=1))
        out = dot(weights[:192, :192], jnp.concatenate([vh, vl], axis=0))
        out = out[:NG] + out[NG:]
        return out[:, :128], out[:, 128:]

    def transform_z(value):
        vh, vl = split(value)
        out = dot(jnp.concatenate([vh, vl], axis=1), weights[192:448, :])
        return out[:, :128] + out[:, 128:]

    def forward(j, t):
        def rows(s, _):
            blk = blk_u[t, across(4 * j + s), :]
            out0, out1 = transform_y(
                orb_u[t, across(2 * s), :] * blk, orb_u[t, across(2 * s + 1), :] * blk
            )
            turned[across(2 * s), :] = out0
            turned[across(2 * s + 1), :] = out1
            return 0

        lax.fori_loop(0, 4, rows, 0, unroll=4)

        def half(h, _):
            out = transform_z(turned[pl.ds(pl.multiple_of(384 * h, 8), 384), :])
            for g in range(4):
                for s in range(3):
                    base = 96 * g + 32 * s
                    tiles = close_quad(*[out[base + 8 * b : base + 8 * b + 8] for b in range(4)])
                    for k in range(3):
                        lane = 384 * s + 128 * k
                        send_a[j, t, 4 * h + g, :, lane : lane + 128] = tiles[k]
            return 0

        lax.fori_loop(0, 2, half, 0)
        for o in range(1, NF):
            copy_a(j, t, turn(o), me).start()
        recv_a[j, t, me] = send_a[j, t, me]

    def middle(j):
        for t in range(NT):
            copy_a(j, t, others, others).wait_recv()

        def step(s, _):
            cols = pl.ds(pl.multiple_of(384 * s, 128), 384)
            value = recv_a[j, :, :, :, cols].reshape(NL * NG, 384)
            spectrum = left_product(weights[448:832, :192], value)
            weight = coulomb[:, cols]
            scaled = jnp.concatenate([spectrum[:NG] * weight, spectrum[NG:] * weight], axis=0)
            back = left_product(weights[832:1216, :192], scaled)
            send_b[j, :, :, :, cols] = back.reshape(NT, NF, 8, 384)
            return 0

        lax.fori_loop(0, 3, step, 0)
        for t in range(NT):
            for o in range(1, NF):
                copy_b(j, t, turn(o), me).start()
            recv_b[j, t, me] = send_b[j, t, me]

    def backward(j, t):
        copy_b(j, t, others, others).wait_recv()

        def half(h, _):
            planes = []
            for g in range(4):
                for s in range(3):
                    planes += open_quad(
                        *[
                            recv_b[j, t, 4 * h + g, :, 384 * s + 128 * k : 384 * s + 128 * k + 128]
                            for k in range(3)
                        ]
                    )
            out = transform_z(jnp.concatenate(planes, axis=0))
            turned[pl.ds(pl.multiple_of(384 * h, 8), 384), :] = out
            return 0

        lax.fori_loop(0, 2, half, 0)

        def rows(s, _):
            even, odd = across(2 * s), across(2 * s + 1)
            pot0, pot1 = transform_y(turned[even, :], turned[odd, :])
            blk = blk_u[t, across(4 * j + s), :]
            term0, term1 = blk * pot0, blk * pot1
            if j > 0:
                term0 = local_u[t, even, :] + term0
                term1 = local_u[t, odd, :] + term1
            local_u[t, even, :] = term0
            local_u[t, odd, :] = term1
            block_u[t, across(4 * j + s), :] = (
                orb_u[t, even, :] * pot0 + orb_u[t, odd, :] * pot1
            )
            return 0

        lax.fori_loop(0, 4, rows, 0, unroll=4)

    def close_block(j, t):
        def step(a, _):
            tiles = close_quad(*[block_u[t, half_plane(4 * a + b, j), :] for b in range(4)])
            for k in range(3):
                source[1, j, t, a // 3, (a % 3) * 3 + k] = tiles[k]
            return 0

        lax.fori_loop(0, QUADS, step, 0, unroll=8)

    def write_local(a, _):
        for t in range(NT):
            tiles = close_quad(*[local_u[t, plane(4 * a + b), :] for b in range(4)])
            for k in range(3):
                lanes = pl.ds(pl.multiple_of(a * 384 + 128 * k, 128), 128)
                local_ref[4 * t : 4 * t + 4, :, lanes] = tiles[k].reshape(4, NL, 128)
        return 0

    def write_half(j, t, piece, first):
        def step(k, _):
            for n in range(PART):
                lanes = pl.ds(pl.multiple_of((9 * k + first + n) * 128, 128), 128)
                block_ref[4 * t : 4 * t + 4, j, lanes] = piece[1, j, t, k, n]
            return 0

        lax.fori_loop(0, NZ, step, 0, unroll=2)

    def receive(j, t):
        sum_f(0, j, t)
        open_blk(j, t)
        forward(j, t)

    def finish(j, t):
        write_half(j, t, total, 4 * core)
        to_mate(1, j, t).wait_recv()
        write_half(j, t, mate, 4 * (1 - core))

    def block_out(t):
        return pltpu.make_async_copy(
            block_ref.at[pl.ds(4 * t, 4)], block_hbm.at[pl.ds(4 * t, 4)], out_sem.at[t]
        )

    sum_c(0, 0, 0)
    sum_c(0, 0, 1)
    sum_b(0, 1, 1)
    sum_c(0, 0, 2)
    sum_d(0, 0, 0)
    sum_b(0, 1, 2)
    sum_c(0, 1, 0)
    sum_d(0, 0, 1)
    sum_d(0, 0, 2)
    sum_e(0, 0, 0)
    sum_d(0, 1, 0)
    receive(0, 0)
    sum_c(0, 1, 1)
    sum_e(0, 0, 1)
    sum_c(0, 1, 2)
    receive(0, 1)
    sum_e(0, 0, 2)
    receive(0, 2)
    sum_d(0, 1, 1)
    sum_d(0, 1, 2)
    sum_e(0, 1, 0)
    receive(1, 0)
    sum_e(0, 1, 1)
    receive(1, 1)
    sum_e(0, 1, 2)
    receive(1, 2)

    def sum_sent(q, j, t):
        to_pair(q, j, t).wait_send()
        to_y(q, j, t).wait_send()
        to_mate(q, j, t).wait_send()
        scatter(q, j, t, others, others).wait_send()
        spread(q, j, t, others, others).wait_send()

    middle(0)
    for j in range(NL):
        for t in range(NT):
            sum_sent(0, j, t)
    middle(1)

    def back(j, t):
        backward(j, t)
        close_block(j, t)
        sum_a(1, j, t)

    back(0, 0)
    sum_b(1, 0, 0)
    back(0, 1)
    sum_b(1, 0, 1)
    back(0, 2)
    sum_b(1, 0, 2)
    sum_c(1, 0, 0)
    back(1, 0)
    sum_b(1, 1, 0)
    sum_c(1, 0, 1)
    back(1, 1)
    sum_b(1, 1, 1)
    sum_c(1, 0, 2)
    sum_d(1, 0, 0)
    back(1, 2)
    lax.fori_loop(0, QUADS // 2, write_local, 0, unroll=2)
    sum_b(1, 1, 2)
    sum_d(1, 0, 1)
    sum_c(1, 1, 0)
    sum_d(1, 0, 2)
    lax.fori_loop(QUADS // 2, QUADS, write_local, 0, unroll=2)
    local_out = pltpu.make_async_copy(local_ref, local_hbm, out_sem.at[NT])
    local_out.start()
    sum_c(1, 1, 1)
    sum_d(1, 1, 0)
    sum_c(1, 1, 2)
    sum_d(1, 1, 1)
    sum_d(1, 1, 2)
    for t in range(NT):
        sum_e(1, 0, t)
    for t in range(NT):
        finish(0, t)
    for j in range(NL):
        for t in range(NT):
            copy_a(j, t, others, others).wait_send()
            copy_b(j, t, others, others).wait_send()
    for t in range(NT):
        sum_e(1, 1, t)
        if t > 0:
            finish(1, t - 1)
            block_out(t - 1).start()
    finish(1, NT - 1)
    block_out(NT - 1).start()
    for j in range(NL):
        for t in range(NT):
            sum_sent(1, j, t)
    local_out.wait()
    for t in range(NT):
        block_out(t).wait()


def per_device(orbitals, owners, cutoff_mask):
    dma = pltpu.SemaphoreType.DMA

    def buffer(*shape):
        return pltpu.VMEM(shape, F32)

    def like(array):
        return pltpu.VMEM(array.shape, array.dtype)

    planes = buffer(NT, PLANES, 128)
    tiles = buffer(2, NL, NT, NZ, 9, 4, 128)
    pieces = buffer(2, NL, NT, NZ, PART, 4, 128)
    single = buffer(2, NL, NT, PART, 4, 128)
    grid = buffer(NL, NT, NF, 8, CHUNK)
    constants = jnp.asarray(tables())
    flat = jax.ShapeDtypeStruct((NX, NL, LANES), F32)
    many = dma((NL, NT))
    few = dma((2, NL, NT))
    anywhere = pl.BlockSpec(memory_space=pl.ANY)
    stay = pl.BlockSpec(memory_space=pltpu.HBM)
    orb = orbitals.transpose(1, 0, 2)
    local, block = pl.pallas_call(
        kernel,
        out_shape=(flat, flat),
        in_specs=[stay, pl.BlockSpec(memory_space=pltpu.SMEM)]
        + [stay] * 2,
        out_specs=(anywhere, anywhere),
        scratch_shapes=[
            like(orb), like(cutoff_mask), like(constants),
            like(flat), like(flat), dma((NT + 2,)), dma((NT + 1,)),
            buffer(NG, CHUNK), tiles, tiles, planes, planes,
            buffer(PLANES, 128), planes, planes, grid, grid, grid, grid,
            pieces, pieces, pieces, single, single, pieces, pieces,
            many, many, many, many, few, few, few, few, few, few, few, few, few, few,
        ],
        compiler_params=pltpu.CompilerParams(
            collective_id=0, has_side_effects=True, vmem_limit_bytes=60 << 20
        ),
    )(orb, owners, cutoff_mask, constants)
    return local.transpose(1, 0, 2), block.transpose(1, 0, 2)


def solution(mesh):
    in_specs = (P("band", "fft", None), P(), P(None, "fft"))
    out_specs = (P("band", "fft", None), P(None, "fft", None))
    return jax.shard_map(
        per_device, mesh=mesh, in_specs=in_specs, out_specs=out_specs, check_vma=False
    )
```
